32 devices in a mesh: band: 2 (over core), plane: 16 (over z, y, x).
Axes of the slice: x: 2, y: 2, z: 4, core: 2. Of those that a mesh axis runs over, the one named last changes fastest.
Arguments:
- bands: float32 [8, 128, 128, 128], P('band', 'plane'), may hold values from -6 to 6
- plan: int32 [2], replicated, may hold values from 0 to 7
Outputs:
- exchange_part: float32 [8, 128, 128, 128], P('band', 'plane')
The draws below stay inside these ranges and needn't reach their ends.
All inputs are finite; a program needn't handle non-finite values.
Results may differ from the reference program's by a relative error of at most 0.00011.
Values sent between devices are 32-bit elements; how exact they have to be, the bound alone decides.
No kernel may reach another device: no remote copies, remote signals or barrier semaphores. Data moves between devices by JAX's collectives and lax.ppermute only.
A program may use at most 64 MiB of HBM per device.

```python
import math
import jax
import jax.numpy as jnp
from jax import lax

NG = 128
STEPS = 2
NB = 8


def shard_levels(own_key, extent, shards, least, top_value):
    def one(axis_at, blocks):
        steps = jax.random.uniform(jax.random.fold_in(jax.random.fold_in(own_key, 6), axis_at), (blocks,), jnp.float32, least / len(shards), top_value / len(shards))
        return jnp.repeat(jnp.exp(steps), extent[axis_at] // blocks).reshape((-1,) + (1,) * (len(extent) - axis_at - 1))

    loudness = one(*shards[0])
    for cut in shards[1:]:
        loudness = loudness * one(*cut)
    return loudness


def noise(stream_key, dims, deviation, bound, shards=(), kind=jnp.bfloat16):
    entries = jax.random.normal(stream_key, dims, jnp.float32) * deviation
    if len(shards) > 0:
        entries = shard_levels(stream_key, dims, shards, -0.22, 0.18) * entries
    return jnp.clip(entries, min=-bound, max=bound).astype(kind)


def setup_inputs(seed: int = 0) -> dict:
    keys = jax.random.split(jax.random.key(seed), 3)
    bands = noise(keys[0], (NB, NG, NG, NG), 1.0, 6.0, ((0, 2), (1, 16)), jnp.float32)
    plan = jax.random.randint(keys[1], (STEPS,), 0, NB).astype(jnp.int32)
    return dict(bands=bands, plan=plan)


screening = 0.1


def coulomb_grid():
    lowest = jnp.arange(NG // 2, dtype=jnp.int32)
    spectral = jnp.concatenate([lowest, lowest - NG // 2])
    squared = spectral[:, None, None] ** 2 + spectral[None, :, None] ** 2 + spectral[None, None, :] ** 2
    spacing = 2.0 * math.pi / NG
    values = 1.0 / (spacing * spacing * squared.astype(jnp.float32) + screening * screening)
    return jnp.where(squared < (NG // 4) ** 2, values, 0.0).astype(jnp.float32)


def reference(bands, plan):
    kernel = coulomb_grid()

    def potential(partner, other_band):
        density = partner * other_band
        spectrum = jnp.fft.fftn(density)
        return jnp.real(jnp.fft.ifftn(spectrum * kernel)).astype(jnp.float32)

    accumulated = jnp.zeros(bands.shape, jnp.float32)
    for turn_index in range(STEPS):
        partner = lax.dynamic_index_in_dim(bands, plan[turn_index], 0, keepdims=False)
        potentials = lax.map(lambda other_band: potential(partner, other_band), bands)
        accumulated = accumulated - partner[None] * potentials
    return accumulated
```

```python
import functools
import math

import jax
import jax.numpy as jnp
import numpy as np
from jax import lax
from jax.experimental import pallas as pl
from jax.experimental.pallas import tpu as pltpu
from jax.sharding import PartitionSpec as P

screening = 0.1
f32 = jnp.float32
bf16 = jnp.bfloat16
vmem_bytes = 56 << 20


def spread(value, axis, source):
    kept = jnp.where(lax.axis_index(axis) == source, value, 0).astype(value.dtype)
    return lax.psum(kept, axis)


def split_host(table):
    high = table.astype(jnp.bfloat16)
    low = (table - high.astype(np.float64)).astype(jnp.bfloat16)
    return high, low


def split(value):
    high = value.astype(bf16)
    return high, (value - high.astype(f32)).astype(bf16)


def dot(left, right):
    return jnp.dot(left, right, preferred_element_type=f32)


def basis(points):
    cutoff = points // 4
    grid = np.arange(points)
    waves = [0] + [k for k in range(1, cutoff) for _ in (0, 1)]
    table = np.zeros((points, 2 * cutoff), np.float64)
    for column, k in enumerate(waves):
        angles = 2.0 * math.pi * (k * grid % points) / points
        values = np.cos(angles) if column % 2 or k == 0 else np.sin(angles)
        table[:, column] = values * math.sqrt((1.0 if k == 0 else 2.0) / points)
    return table, waves


def layout(points, planes, plane_count, bands):
    table, waves = basis(points)
    slots = table.shape[1]
    far = float(points * points)
    squares = np.array([float(k * k) for k in waves] + [far])
    rows = slots
    units = bands * rows // plane_count
    lanes = squares[:, None] + squares[None, :]
    lanes = np.concatenate([lanes, lanes], 1)
    return table, squares, rows, units, lanes.astype(np.float32)


def forward_kernel(info, band, own0, own1, met0, met1, ztable, zlow, ytable, out, partner):
    planes, points = band.shape[1], band.shape[2]
    rows = ytable.shape[0] // 2

    @pl.when(pl.program_id(0) == 0)
    def _():
        for turn, (own, met) in enumerate(((own0, met0), (own1, met1))):
            @pl.when(info[2 + turn] == 1)
            def _():
                partner[turn] = own[0]

            @pl.when(info[2 + turn] == 0)
            def _():
                partner[turn] = met[0]

    step = 2
    for start in range(0, planes, step):
        here = band[0, start : start + step]
        density = jnp.concatenate(
            [partner[0, start : start + step] * here, partner[1, start : start + step] * here], 2
        ).reshape(step * points, 2 * points)
        high, low = split(density)
        both = dot(high, ztable[...])
        half = both.shape[1] // 2
        lines = both[:, :half] + both[:, half:] + dot(low, zlow[...])
        lines = jnp.concatenate([lines[at * points : (at + 1) * points] for at in range(step)], 1)
        high, low = split(lines)
        both = dot(ytable[...], jnp.concatenate([high, low], 0))
        columns = both[:rows] + both[rows:]
        for at in range(step):
            out[0, pl.ds(start + at, rows, stride=planes), :] = columns[:, at * half : (at + 1) * half]


def middle_kernel(info, got, lanes, wave, xtable, xback, out, *, planes, points):
    group = 8 // planes
    tiles = got.shape[1] // 8
    kept = xtable.shape[0] // 2
    spacing = 2.0 * math.pi / points
    cutoff = float((points // 4) ** 2)
    width = got.shape[2]
    for first in range(0, tiles, 2):
        count = min(2, tiles - first)
        values = jnp.concatenate(
            [got[:, 8 * at : 8 * at + 8, :].reshape(-1, width) for at in range(first, first + count)], 1
        )
        high, low = split(values)
        both = dot(xtable[...], jnp.concatenate([high, low], 0))
        spectrum = both[:kept] + both[kept:]
        factor = []
        for at in range(first, first + count):
            parts = []
            for item in range(group):
                unit = at * group + item
                squared = wave[...] + lanes[0, unit : unit + 1, :]
                weight = 1.0 / (spacing * spacing * squared + screening * screening)
                parts.append(jnp.where(squared < cutoff, weight, 0.0))
            factor.append(parts[0] if group == 1 else jnp.concatenate(parts, 0))
        spectrum = spectrum * (factor[0] if count == 1 else jnp.concatenate(factor, 1))
        high, low = split(spectrum)
        back = dot(xback[...], jnp.concatenate([high, low, high], 0))
        for at in range(count):
            piece = back[:, at * width : (at + 1) * width]
            out[:, 8 * (first + at) : 8 * (first + at) + 8, :] = piece.reshape(-1, 8, width)


def backward_kernel(got, partner, yback, zback, zlow, out):
    planes, points = out.shape[1], out.shape[2]
    rows = yback.shape[1] // 3
    width = got.shape[2]
    step = 2
    for start in range(0, planes, step):
        columns = jnp.concatenate(
            [got[0, pl.ds(start + at, rows, stride=planes), :] for at in range(step)], 1
        )
        high, low = split(columns)
        lines = dot(yback[...], jnp.concatenate([high, low, high], 0))
        lines = jnp.concatenate([lines[:, at * width : (at + 1) * width] for at in range(step)], 0)
        high, low = split(lines)
        waves = dot(jnp.concatenate([high, low], 1), zback[...]) + dot(high, zlow[...])
        waves = waves.reshape(step, points, 2 * points)
        out[0, start : start + step] = -(
            partner[0, start : start + step] * waves[:, :, :points]
            + partner[1, start : start + step] * waves[:, :, points:]
        )


def per_device(bands, plan, band_count, plane_count):
    count, planes, points = bands.shape[0], bands.shape[1], bands.shape[2]
    assert plan.shape[0] == 2 and 8 % planes == 0
    table, squares, rows, units, lanes = layout(points, planes, plane_count, count)
    slots = table.shape[1]
    width = 2 * slots
    high, low = split_host(table)
    zero = np.zeros_like(high)

    own_index = plan % count
    mine = (plan // count == lax.axis_index("band")).astype(jnp.int32)
    own = [lax.dynamic_index_in_dim(bands, own_index[turn], 0) for turn in range(2)]
    if band_count == 2:
        met = [lax.ppermute(own[turn], "band", [(0, 1), (1, 0)]) for turn in range(2)]
    else:
        met = [spread(own[turn], "band", plan[turn] // count) for turn in range(2)]
    info = jnp.concatenate([own_index, mine]).astype(jnp.int32)

    def pair(block):
        empty = np.zeros_like(block)
        return np.block([[block, empty], [empty, block]])

    z_high, z_low = pair(high), pair(low)
    forward_z = jnp.asarray(np.concatenate([z_high, z_low], 1))
    forward_y = jnp.asarray(np.block([[high.T, high.T], [low.T, zero.T]]))
    block4 = (1, planes, points, points)
    whole = lambda *shape: pl.BlockSpec(shape, lambda i, s: (0,) * len(shape))
    sent, partner = pl.pallas_call(
        forward_kernel,
        out_shape=(
            jax.ShapeDtypeStruct((count, rows * planes, width), f32),
            jax.ShapeDtypeStruct((2, planes, points, points), f32),
        ),
        grid_spec=pltpu.PrefetchScalarGridSpec(
            num_scalar_prefetch=1,
            grid=(count,),
            in_specs=[
                pl.BlockSpec(block4, lambda i, s: (i, 0, 0, 0)),
                pl.BlockSpec(block4, lambda i, s: (s[0], 0, 0, 0)),
                pl.BlockSpec(block4, lambda i, s: (s[1], 0, 0, 0)),
                whole(*block4),
                whole(*block4),
                whole(2 * points, 2 * width),
                whole(2 * points, width),
                whole(2 * rows, 2 * points),
            ],
            out_specs=(
                pl.BlockSpec((1, rows * planes, width), lambda i, s: (i, 0, 0)),
                whole(2, planes, points, points),
            ),
        ),
        compiler_params=pltpu.CompilerParams(vmem_limit_bytes=vmem_bytes),
        name="forward",
    )(info, bands, bands, bands, met[0], met[1], forward_z, jnp.asarray(z_high), forward_y)

    lines = units * planes
    got = lax.all_to_all(
        sent.reshape(plane_count, lines, width), "plane", split_axis=0, concat_axis=0, tiled=True
    )

    group = 8 // planes
    place = np.zeros((group * slots, plane_count * 8), np.float64)
    for item in range(group):
        for source in range(plane_count):
            for plane in range(planes):
                place[item * slots : (item + 1) * slots, source * 8 + item * planes + plane] = table[
                    source * planes + plane
                ]
    x_high, x_low = split_host(place)
    forward_x = jnp.asarray(np.block([[x_high, x_high], [x_low, np.zeros_like(x_low)]]))
    backward_x = jnp.asarray(np.concatenate([x_high.T, x_high.T, x_low.T], 1))
    quarters = rows // units
    where_rows = (lax.axis_index("plane") % quarters).astype(jnp.int32)[None]
    wave = jnp.asarray(np.tile(squares.astype(np.float32)[:, None], (1, width)))
    back = pl.pallas_call(
        functools.partial(middle_kernel, planes=planes, points=points),
        out_shape=jax.ShapeDtypeStruct((plane_count, lines, width), f32),
        grid_spec=pltpu.PrefetchScalarGridSpec(
            num_scalar_prefetch=1,
            grid=(1,),
            in_specs=[
                whole(plane_count, lines, width),
                pl.BlockSpec((1, units, width), lambda i, s: (s[0], 0, 0)),
                whole(slots, width),
                whole(*forward_x.shape),
                whole(*backward_x.shape),
            ],
            out_specs=whole(plane_count, lines, width),
        ),
        compiler_params=pltpu.CompilerParams(vmem_limit_bytes=vmem_bytes),
        name="middle",
    )(where_rows, got, jnp.asarray(lanes.reshape(quarters, units, width)), wave, forward_x, backward_x)
    home = lax.all_to_all(back, "plane", split_axis=0, concat_axis=0, tiled=True)
    home = home.reshape(count, rows * planes, width)

    backward_y = jnp.asarray(np.concatenate([high, high, low], 1))
    back_high, back_low = pair(high.T), pair(low.T)
    backward_z = jnp.asarray(np.concatenate([back_high, back_high], 0))
    all1 = lambda *shape: pl.BlockSpec(shape, lambda i: (0,) * len(shape))
    return pl.pallas_call(
        backward_kernel,
        out_shape=jax.ShapeDtypeStruct(bands.shape, f32),
        grid=(count,),
        in_specs=[
            pl.BlockSpec((1, rows * planes, width), lambda i: (i, 0, 0)),
            all1(2, planes, points, points),
            all1(*backward_y.shape),
            all1(*backward_z.shape),
            all1(*back_low.shape),
        ],
        out_specs=pl.BlockSpec(block4, lambda i: (i, 0, 0, 0)),
        compiler_params=pltpu.CompilerParams(vmem_limit_bytes=vmem_bytes),
        name="backward",
    )(home, partner, backward_y, backward_z, jnp.asarray(back_low))


def solution(mesh):
    in_specs = (P("band", "plane", None, None), P())
    out_specs = P("band", "plane", None, None)
    body = functools.partial(
        per_device, band_count=mesh.shape["band"], plane_count=mesh.shape["plane"]
    )
    return jax.shard_map(
        body, mesh=mesh, in_specs=in_specs, out_specs=out_specs, check_vma=False
    )
```

```python
import functools
import math

import jax
import jax.numpy as jnp
import numpy as np
from jax import lax
from jax.experimental import pallas as pl
from jax.experimental.pallas import tpu as pltpu
from jax.sharding import PartitionSpec as P

screening = 0.1
f32 = jnp.float32
bf16 = jnp.bfloat16
vmem_bytes = 24 << 20


def spread(value, axis, source):
    kept = jnp.where(lax.axis_index(axis) == source, value, 0).astype(value.dtype)
    return lax.psum(kept, axis)


def split_host(table):
    high = table.astype(jnp.bfloat16)
    low = (table - high.astype(np.float64)).astype(jnp.bfloat16)
    return high, low


def split(value):
    high = value.astype(bf16)
    return high, (value - high.astype(f32)).astype(bf16)


def dot(left, right):
    return jnp.dot(left, right, preferred_element_type=f32)


def basis(points):
    cutoff = points // 4
    grid = np.arange(points)
    waves = [k for k in range(1, cutoff) for _ in (0, 1)] + [0]
    table = np.zeros((points, 2 * cutoff), np.float64)
    for column, k in enumerate(waves):
        angles = 2.0 * math.pi * (k * grid % points) / points
        values = np.sin(angles) if column % 2 else np.cos(angles)
        table[:, column] = values * math.sqrt((1.0 if k == 0 else 2.0) / points)
    return table, waves


class Packing:
    def __init__(self, points, rows):
        table, waves = basis(points)
        cutoff = points // 4
        slots = 2 * cutoff
        order = sorted(range(slots - 1), key=lambda f: waves[f])
        self.ztable = np.concatenate([table[:, order], np.zeros((points, 1))], 1)
        zsquares = np.array([float(waves[f] ** 2) for f in order] + [np.inf])
        used = lambda k: int(np.sum(zsquares + k * k < cutoff**2))
        pairs = cutoff - 1 if rows == slots else (rows - 1) // 2
        self.rows = rows
        self.tall = tall = -(-rows // 8)
        base = lambda h: min(8 * h, rows - 8)
        self.base = base
        spot = lambda row: (row // 8, row - base(row // 8))
        far = float(points * points)
        squares = np.full((rows, slots), far)
        host = np.zeros((8 * tall,), np.int64) - 1
        owner = np.full((8 * tall, slots), -1)
        free = []

        def place(function, row, start, length, at):
            squares[row, at : at + length] = waves[function] ** 2 + zsquares[start : start + length]

        def settle(function, row):
            h, s = spot(row)
            host[8 * h + s] = function
            length = used(waves[function])
            owner[8 * h + s, :length] = 0
            place(function, row, 0, length, 0)
            return length

        for k in range(1, pairs + 1):
            for part in (0, 1):
                length = settle(2 * k - 2 + part, 2 * k - 2 + part)
            free.append([2 * k - 2, length, slots - length])
        settle(slots - 2, 2 * pairs)
        blank = 2 * pairs + 1 if 2 * pairs + 1 < rows else None

        extra = []
        moves = {}
        cells = []

        def move(function, row, start, at, length):
            h, s = spot(row)
            for e, held in enumerate(extra):
                if held[s] in (-1, function):
                    break
            else:
                e = len(extra)
                extra.append([-1] * 8)
            extra[e][s] = function
            number = moves.setdefault((e, h, (at - start) % (2 * slots)), len(moves) + 1)
            owner[8 * h + s, at : at + length] = number
            cells.append((number, e, s, start, length))
            place(function, row, start, length, at)

        rest = {k: [0, used(k)] for k in range(pairs + 1, cutoff)}

        def take(k, length, row, at, both):
            start = rest[k][0]
            for part in (0, 1):
                if both:
                    move(2 * k - 2 + part, row + part, start, at, length)
                else:
                    move(2 * k - 2 + part, row, start, at + part * (slots // 2), length)
            rest[k] = [start + length, rest[k][1] - length]
            if rest[k][1] == 0:
                del rest[k]

        gaps = [[length, row, at, True] for row, at, length in free]
        if blank is not None:
            gaps.append([slots // 2, blank, 0, False])
        gaps.sort(reverse=True)
        while rest:
            exact = [(g, k) for g in gaps for k in rest if rest[k][1] == g[0]]
            if exact:
                gap, k = exact[0]
            else:
                k = max(rest, key=lambda k: rest[k][1])
                whole = [g for g in gaps if g[0] >= rest[k][1]]
                gap = min(whole) if whole else gaps[0]
            length = min(gap[0], rest[k][1])
            take(k, length, gap[1], gap[2], gap[3])
            gap[0] -= length
            gap[2] += length
            gaps.sort(reverse=True)

        while (8 * tall + 8 * len(extra)) % 16:
            extra.append([-1] * 8)
        self.moves = [(number, e, h, shift) for (e, h, shift), number in moves.items()]
        self.extra = len(extra)
        came = np.full((8 * len(extra), slots), -1)
        for number, e, s, start, length in cells:
            came[8 * e + s, start : start + length] = number
        twice = lambda a: np.concatenate([a, a], 1)
        self.owner = twice(owner).astype(np.int32)
        self.came = twice(came).astype(np.int32) if extra else np.zeros((8, 2 * slots), np.int32)
        functions = list(host) + [f for held in extra for f in held]
        self.ytable = np.stack([table[:, f] if f >= 0 else np.zeros(points) for f in functions])
        self.lanes = twice(squares).astype(np.float32)
        self.table = table
        self.squares = np.array([float(k * k) for k in waves] + [far], np.float32)


def forward_kernel(info, bands, met, ztable, zlow, ytable, owner, out, partner, *, pack):
    count, planes, points = bands.shape[:3]
    tall, width = ytable.shape[0] // 2, zlow.shape[1]
    for turn in range(2):
        @pl.when(info[2 + turn] == 1)
        def _():
            partner[turn] = bands[info[turn]]

        @pl.when(info[2 + turn] == 0)
        def _():
            partner[turn] = met[info[4 + turn]]

    def one(band, carry):
        step = 2
        for start in range(0, planes, step):
            here = bands[band, start : start + step]
            density = jnp.concatenate(
                [partner[0, start : start + step] * here, partner[1, start : start + step] * here], 2
            ).reshape(step * points, 2 * points)
            high, low = split(density)
            both = dot(high, ztable[...])
            lines = both[:, :width] + both[:, width:] + dot(low, zlow[...])
            lines = jnp.concatenate([lines[at * points : (at + 1) * points] for at in range(step)], 1)
            high, low = split(lines)
            both = dot(ytable[...], jnp.concatenate([high, low], 0))
            columns = both[:tall] + both[tall:]
            for at in range(step):
                mine = columns[:, at * width : (at + 1) * width]
                host = [mine[8 * h : 8 * h + 8] for h in range(pack.tall)]
                more = [mine[8 * (pack.tall + e) : 8 * (pack.tall + e) + 8] for e in range(pack.extra)]
                for number, e, h, shift in pack.moves:
                    rolled = pltpu.roll(more[e], shift, 1) if shift else more[e]
                    host[h] = jnp.where(owner[8 * h : 8 * h + 8, :] == number, rolled, host[h])
                for h in reversed(range(pack.tall)):
                    first = pack.base(h) * planes + start + at
                    out[band, pl.ds(first, 8, stride=planes), :] = host[h]
        return carry

    lax.fori_loop(0, count, one, 0)


def middle_kernel(got, lanes, wave, xtable, xback, out, *, planes, points):
    group = 8 // planes
    tiles = got.shape[1] // 8
    kept = xtable.shape[0] // 2
    spacing = 2.0 * math.pi / points
    cutoff = float((points // 4) ** 2)
    width = got.shape[2]
    for first in range(0, tiles, 2):
        count = min(2, tiles - first)
        values = jnp.concatenate(
            [got[:, 8 * at : 8 * at + 8, :].reshape(-1, width) for at in range(first, first + count)], 1
        )
        high, low = split(values)
        both = dot(xtable[...], jnp.concatenate([high, low], 0))
        spectrum = both[:kept] + both[kept:]
        factor = []
        for at in range(first, first + count):
            parts = []
            for item in range(group):
                unit = at * group + item
                squared = wave[...] + lanes[unit : unit + 1, :]
                weight = 1.0 / (spacing * spacing * squared + screening * screening)
                parts.append(jnp.where(squared < cutoff, weight, 0.0))
            factor.append(parts[0] if group == 1 else jnp.concatenate(parts, 0))
        spectrum = spectrum * (factor[0] if count == 1 else jnp.concatenate(factor, 1))
        high, low = split(spectrum)
        back = dot(xback[...], jnp.concatenate([high, low, high], 0))
        for at in range(count):
            piece = back[:, at * width : (at + 1) * width]
            out[:, 8 * (first + at) : 8 * (first + at) + 8, :] = piece.reshape(-1, 8, width)


def backward_kernel(got, partner, yback, zback, zlow, owner, came, out, *, pack):
    planes, points = out.shape[1], out.shape[2]
    width = got.shape[2]
    step = 2

    def spectrum(plane):
        whole = [
            got[0, pl.ds(pack.base(h) * planes + plane, 8, stride=planes), :] for h in range(pack.tall)
        ]
        more = [jnp.zeros((8, width), f32) for _ in range(pack.extra)]
        for number, e, h, shift in pack.moves:
            rolled = pltpu.roll(whole[h], width - shift, 1) if shift else whole[h]
            more[e] = jnp.where(came[8 * e : 8 * e + 8, :] == number, rolled, more[e])
        host = [jnp.where(owner[8 * h : 8 * h + 8, :] == 0, whole[h], 0.0) for h in range(pack.tall)]
        return jnp.concatenate(host + more, 0)

    for start in range(0, planes, step):
        columns = jnp.concatenate([spectrum(start + at) for at in range(step)], 1)
        high, low = split(columns)
        lines = dot(yback[...], jnp.concatenate([high, low, high], 0))
        lines = jnp.concatenate([lines[:, at * width : (at + 1) * width] for at in range(step)], 0)
        high, low = split(lines)
        waves = dot(jnp.concatenate([high, low], 1), zback[...]) + dot(high, zlow[...])
        waves = waves.reshape(step, points, 2 * points)
        out[0, start : start + step] = -(
            partner[0, start : start + step] * waves[:, :, :points]
            + partner[1, start : start + step] * waves[:, :, points:]
        )


def in_vmem(value):
    return pltpu.with_memory_space_constraint(value, pltpu.VMEM)


def per_device(bands, plan, band_count, plane_count):
    count, planes, points = bands.shape[0], bands.shape[1], bands.shape[2]
    assert plan.shape[0] == 2 and 8 % planes == 0
    for rows in (52, 56, 60, 64):
        if points == 128 and count * rows % plane_count == 0 and rows % (count * rows // plane_count) == 0:
            units = count * rows // plane_count
            if units * planes % 8 == 0:
                break
    pack = Packing(points, rows)
    slots = pack.table.shape[1]
    width = 2 * slots
    vmem = pl.BlockSpec(memory_space=pltpu.VMEM)

    own_index = plan % count
    owner_group = plan // count
    if band_count == 2:
        met = lax.ppermute(bands, "band", [(0, 1), (1, 0)])
        met_index = own_index
    else:
        met = jnp.stack(
            [
                spread(lax.dynamic_index_in_dim(bands, own_index[turn], 0, False), "band", owner_group[turn])
                for turn in range(2)
            ]
        )
        met_index = jnp.arange(2, dtype=jnp.int32)
    mine = (owner_group == lax.axis_index("band")).astype(jnp.int32)
    info = jnp.concatenate([own_index, mine, met_index]).astype(jnp.int32)

    def pair(block):
        empty = np.zeros_like(block)
        return np.block([[block, empty], [empty, block]])

    z_high, z_low = split_host(pack.ztable)
    y_high, y_low = split_host(pack.ytable)
    forward_z = jnp.asarray(np.concatenate([pair(z_high), pair(z_low)], 1))
    forward_y = jnp.asarray(np.block([[y_high, y_high], [y_low, np.zeros_like(y_low)]]))
    owner = jnp.asarray(pack.owner)
    sent, partner = pl.pallas_call(
        functools.partial(forward_kernel, pack=pack),
        out_shape=(
            pltpu.VMEM((count, rows * planes, width), f32),
            pltpu.VMEM((2, planes, points, points), f32),
        ),
        in_specs=[pl.BlockSpec(memory_space=pltpu.SMEM)] + [vmem] * 6,
        out_specs=(vmem, vmem),
        compiler_params=pltpu.CompilerParams(vmem_limit_bytes=vmem_bytes),
        name="forward",
    )(info, in_vmem(bands), in_vmem(met), forward_z, jnp.asarray(pair(z_high)), forward_y, owner)

    lines = units * planes
    got = lax.all_to_all(
        sent.reshape(plane_count, lines, width), "plane", split_axis=0, concat_axis=0, tiled=True
    )

    group = 8 // planes
    place = np.zeros((group * slots, plane_count * 8), np.float64)
    for item in range(group):
        for source in range(plane_count):
            for plane in range(planes):
                place[item * slots : (item + 1) * slots, source * 8 + item * planes + plane] = pack.table[
                    source * planes + plane
                ]
    x_high, x_low = split_host(place)
    forward_x = jnp.asarray(np.block([[x_high, x_high], [x_low, np.zeros_like(x_low)]]))
    backward_x = jnp.asarray(np.concatenate([x_high.T, x_high.T, x_low.T], 1))
    quarters = rows // units
    lanes = lax.dynamic_index_in_dim(
        jnp.asarray(pack.lanes.reshape(quarters, units, width)), lax.axis_index("plane") % quarters, 0, False
    )
    wave = jnp.asarray(np.tile(pack.squares[:, None], (1, width)))
    back = pl.pallas_call(
        functools.partial(middle_kernel, planes=planes, points=points),
        out_shape=pltpu.VMEM((plane_count, lines, width), f32),
        in_specs=[vmem] * 5,
        out_specs=vmem,
        compiler_params=pltpu.CompilerParams(vmem_limit_bytes=vmem_bytes),
        name="middle",
    )(in_vmem(got), lanes, wave, forward_x, backward_x)
    home = lax.all_to_all(back, "plane", split_axis=0, concat_axis=0, tiled=True)
    home = home.reshape(count, rows * planes, width)

    backward_y = jnp.asarray(np.concatenate([y_high.T, y_high.T, y_low.T], 1))
    back_high, back_low = pair(z_high.T), pair(z_low.T)
    backward_z = jnp.asarray(np.concatenate([back_high, back_high], 0))
    block4 = (1, planes, points, points)
    all1 = lambda *shape: pl.BlockSpec(shape, lambda i: (0,) * len(shape))
    return pl.pallas_call(
        functools.partial(backward_kernel, pack=pack),
        out_shape=jax.ShapeDtypeStruct(bands.shape, f32),
        grid=(count,),
        in_specs=[
            pl.BlockSpec((1, rows * planes, width), lambda i: (i, 0, 0)),
            all1(2, planes, points, points),
            all1(*backward_y.shape),
            all1(*backward_z.shape),
            all1(*back_low.shape),
            all1(*pack.owner.shape),
            all1(*pack.came.shape),
        ],
        out_specs=pl.BlockSpec(block4, lambda i: (i, 0, 0, 0)),
        compiler_params=pltpu.CompilerParams(vmem_limit_bytes=vmem_bytes),
        name="backward",
    )(home, partner, backward_y, backward_z, jnp.asarray(back_low), owner, jnp.asarray(pack.came))


def solution(mesh):
    in_specs = (P("band", "plane", None, None), P())
    out_specs = P("band", "plane", None, None)
    body = functools.partial(
        per_device, band_count=mesh.shape["band"], plane_count=mesh.shape["plane"]
    )
    return jax.shard_map(
        body, mesh=mesh, in_specs=in_specs, out_specs=out_specs, check_vma=False
    )
```

```python
import functools
import math

import jax
import jax.numpy as jnp
import numpy as np
from jax import lax
from jax.experimental import pallas as pl
from jax.experimental.pallas import tpu as pltpu
from jax.sharding import PartitionSpec as P

screening = 0.1
f32 = jnp.float32
bf16 = jnp.bfloat16
vmem_bytes = 24 << 20


def spread(value, axis, source):
    kept = jnp.where(lax.axis_index(axis) == source, value, 0).astype(value.dtype)
    return lax.psum(kept, axis)


def split_host(table):
    high = table.astype(jnp.bfloat16)
    low = (table - high.astype(np.float64)).astype(jnp.bfloat16)
    return high, low


def split(value):
    high = value.astype(bf16)
    return high, (value - high.astype(f32)).astype(bf16)


def dot(left, right):
    return jnp.dot(left, right, preferred_element_type=f32)


def basis(points):
    cutoff = points // 4
    grid = np.arange(points)
    waves = [k for k in range(1, cutoff) for _ in (0, 1)] + [0]
    table = np.zeros((points, 2 * cutoff), np.float64)
    for column, k in enumerate(waves):
        angles = 2.0 * math.pi * (k * grid % points) / points
        values = np.sin(angles) if column % 2 else np.cos(angles)
        table[:, column] = values * math.sqrt((1.0 if k == 0 else 2.0) / points)
    return table, waves


class Packing:
    def __init__(self, points, rows):
        table, waves = basis(points)
        cutoff = points // 4
        slots = 2 * cutoff
        order = sorted(range(slots - 1), key=lambda f: waves[f])
        self.ztable = np.concatenate([table[:, order], np.zeros((points, 1))], 1)
        zsquares = np.array([float(waves[f] ** 2) for f in order] + [np.inf])
        used = lambda k: int(np.sum(zsquares + k * k < cutoff**2))
        pairs = cutoff - 1 if rows == slots else (rows - 1) // 2
        self.rows = rows
        self.tall = tall = -(-rows // 8)
        base = lambda h: min(8 * h, rows - 8)
        self.base = base
        spot = lambda row: (row // 8, row - base(row // 8))
        far = float(points * points)
        squares = np.full((rows, slots), far)
        host = np.zeros((8 * tall,), np.int64) - 1
        owner = np.full((8 * tall, slots), -1)
        free = []

        def place(function, row, start, length, at):
            squares[row, at : at + length] = waves[function] ** 2 + zsquares[start : start + length]

        def settle(function, row):
            h, s = spot(row)
            host[8 * h + s] = function
            length = used(waves[function])
            owner[8 * h + s, :length] = 0
            place(function, row, 0, length, 0)
            return length

        for k in range(1, pairs + 1):
            for part in (0, 1):
                length = settle(2 * k - 2 + part, 2 * k - 2 + part)
            free.append([2 * k - 2, length, slots - length])
        settle(slots - 2, 2 * pairs)
        blank = 2 * pairs + 1 if 2 * pairs + 1 < rows else None

        extra = []
        moves = {}
        cells = []

        def move(function, row, start, at, length):
            h, s = spot(row)
            for e, held in enumerate(extra):
                if held[s] in (-1, function):
                    break
            else:
                e = len(extra)
                extra.append([-1] * 8)
            extra[e][s] = function
            number = moves.setdefault((e, h, (at - start) % (2 * slots)), len(moves) + 1)
            owner[8 * h + s, at : at + length] = number
            cells.append((number, e, s, start, length))
            place(function, row, start, length, at)

        rest = {k: [0, used(k)] for k in range(pairs + 1, cutoff)}

        def take(k, length, row, at, both):
            start = rest[k][0]
            for part in (0, 1):
                if both:
                    move(2 * k - 2 + part, row + part, start, at, length)
                else:
                    move(2 * k - 2 + part, row, start, at + part * (slots // 2), length)
            rest[k] = [start + length, rest[k][1] - length]
            if rest[k][1] == 0:
                del rest[k]

        gaps = [[length, row, at, True] for row, at, length in free]
        if blank is not None:
            gaps.append([slots // 2, blank, 0, False])
        gaps.sort(reverse=True)
        while rest:
            exact = [(g, k) for g in gaps for k in rest if rest[k][1] == g[0]]
            if exact:
                gap, k = exact[0]
            else:
                k = max(rest, key=lambda k: rest[k][1])
                whole = [g for g in gaps if g[0] >= rest[k][1]]
                gap = min(whole) if whole else gaps[0]
            length = min(gap[0], rest[k][1])
            take(k, length, gap[1], gap[2], gap[3])
            gap[0] -= length
            gap[2] += length
            gaps.sort(reverse=True)

        while (8 * tall + 8 * len(extra)) % 16:
            extra.append([-1] * 8)
        self.moves = [(number, e, h, shift) for (e, h, shift), number in moves.items()]
        self.extra = len(extra)
        came = np.full((8 * len(extra), slots), -1)
        for number, e, s, start, length in cells:
            came[8 * e + s, start : start + length] = number
        twice = lambda a: np.concatenate([a, a], 1)
        self.owner = twice(owner).astype(np.int32)
        self.came = twice(came).astype(np.int32) if extra else np.zeros((8, 2 * slots), np.int32)
        functions = list(host) + [f for held in extra for f in held]
        self.ytable = np.stack([table[:, f] if f >= 0 else np.zeros(points) for f in functions])
        self.lanes = twice(squares).astype(np.float32)
        self.table = table
        self.squares = np.array([float(k * k) for k in waves] + [far], np.float32)


def load_kernel(*refs):
    count = len(refs) // 2
    sems = refs[-1]
    copies = [
        pltpu.make_async_copy(source, target, sems.at[at])
        for at, (source, target) in enumerate(zip(refs[:count], refs[count : 2 * count]))
    ]
    for copy in copies:
        copy.start()
    for copy in copies:
        copy.wait()


def load(values):
    return pl.pallas_call(
        load_kernel,
        out_shape=tuple(pltpu.VMEM(v.shape, v.dtype) for v in values),
        in_specs=[pl.BlockSpec(memory_space=pltpu.HBM)] * len(values),
        out_specs=(pl.BlockSpec(memory_space=pltpu.VMEM),) * len(values),
        scratch_shapes=[pltpu.SemaphoreType.DMA((len(values),))],
        cost_estimate=pl.CostEstimate(
            flops=0, transcendentals=0, bytes_accessed=2 * sum(v.size * v.dtype.itemsize for v in values)
        ),
        compiler_params=pltpu.CompilerParams(vmem_limit_bytes=vmem_bytes),
        name="load",
    )(*[pltpu.with_memory_space_constraint(v, pltpu.HBM) for v in values])


def forward_kernel(info, bands, met, ztable, ytable, owner, lanes, out, partner, mine, *, pack, step):
    count, planes, points = bands.shape[:3]
    tall, width = ytable.shape[0] // 2, ztable.shape[1] // 2
    mine[...] = lanes[info[6]]
    for turn in range(2):
        @pl.when(info[2 + turn] == 1)
        def _():
            partner[turn] = bands[info[turn]]

        @pl.when(info[2 + turn] == 0)
        def _():
            partner[turn] = met[info[4 + turn]]

    def one(band, carry):
        for start in range(0, planes, step):
            here = bands[band, start : start + step]
            density = jnp.concatenate(
                [partner[0, start : start + step] * here, partner[1, start : start + step] * here], 2
            ).reshape(step * points, 2 * points)
            high, low = split(density)
            both = dot(high, ztable[...])
            lines = both[:, :width] + both[:, width:] + dot(low, ztable[:, :width])
            lines = jnp.concatenate([lines[at * points : (at + 1) * points] for at in range(step)], 1)
            high, low = split(lines)
            both = dot(ytable[...], jnp.concatenate([high, low], 0))
            columns = both[:tall] + both[tall:]
            for at in range(step):
                piece = columns[:, at * width : (at + 1) * width]
                host = [piece[8 * h : 8 * h + 8] for h in range(pack.tall)]
                more = [piece[8 * (pack.tall + e) : 8 * (pack.tall + e) + 8] for e in range(pack.extra)]
                for number, e, h, shift in pack.moves:
                    rolled = pltpu.roll(more[e], shift, 1) if shift else more[e]
                    host[h] = jnp.where(owner[8 * h : 8 * h + 8, :] == number, rolled, host[h])
                for h in reversed(range(pack.tall)):
                    first = pack.base(h) * planes + start + at
                    out[band, pl.ds(first, 8, stride=planes), :] = host[h]
        return carry

    lax.fori_loop(0, count, one, 0)


def middle_kernel(got, lanes, wave, xtable, xback, out, *, planes, points):
    group = 8 // planes
    tiles = got.shape[1] // 8
    kept = xtable.shape[0] // 2
    spacing = 2.0 * math.pi / points
    cutoff = float((points // 4) ** 2)
    width = got.shape[2]
    for first in range(0, tiles, 2):
        count = min(2, tiles - first)
        values = jnp.concatenate(
            [got[:, 8 * at : 8 * at + 8, :].reshape(-1, width) for at in range(first, first + count)], 1
        )
        high, low = split(values)
        both = dot(xtable[...], jnp.concatenate([high, low], 0))
        spectrum = both[:kept] + both[kept:]
        factor = []
        for at in range(first, first + count):
            parts = []
            for item in range(group):
                unit = at * group + item
                squared = wave[...] + lanes[unit : unit + 1, :]
                weight = 1.0 / (spacing * spacing * squared + screening * screening)
                parts.append(jnp.where(squared < cutoff, weight, 0.0))
            factor.append(parts[0] if group == 1 else jnp.concatenate(parts, 0))
        spectrum = spectrum * (factor[0] if count == 1 else jnp.concatenate(factor, 1))
        high, low = split(spectrum)
        back = dot(xback[...], jnp.concatenate([high, low, high], 0))
        for at in range(count):
            piece = back[:, at * width : (at + 1) * width]
            out[:, 8 * (first + at) : 8 * (first + at) + 8, :] = piece.reshape(-1, 8, width)


def backward_kernel(got, partner, yback, zback, zlow, owner, came, out, *, pack, step):
    planes, points = out.shape[1], out.shape[2]
    width = got.shape[2]

    def spectrum(plane):
        whole = [
            got[pl.program_id(0), pl.ds(pack.base(h) * planes + plane, 8, stride=planes), :] for h in range(pack.tall)
        ]
        more = [jnp.zeros((8, width), f32) for _ in range(pack.extra)]
        for number, e, h, shift in pack.moves:
            rolled = pltpu.roll(whole[h], width - shift, 1) if shift else whole[h]
            more[e] = jnp.where(came[8 * e : 8 * e + 8, :] == number, rolled, more[e])
        host = [jnp.where(owner[8 * h : 8 * h + 8, :] == 0, whole[h], 0.0) for h in range(pack.tall)]
        return jnp.concatenate(host + more, 0)

    for start in range(0, planes, step):
        columns = jnp.concatenate([spectrum(start + at) for at in range(step)], 1)
        high, low = split(columns)
        lines = dot(yback[...], jnp.concatenate([high, low], 0))
        lines = lines[:points] + lines[points:]
        lines = jnp.concatenate([lines[:, at * width : (at + 1) * width] for at in range(step)], 0)
        high, low = split(lines)
        waves = dot(jnp.concatenate([high, low], 1), zback[...]) + dot(high, zlow[...])
        waves = waves.reshape(step, points, 2 * points)
        out[0, start : start + step] = -(
            partner[0, start : start + step] * waves[:, :, :points]
            + partner[1, start : start + step] * waves[:, :, points:]
        )


def in_vmem(value):
    return pltpu.with_memory_space_constraint(value, pltpu.VMEM)


def per_device(bands, plan, band_count, plane_count):
    count, planes, points = bands.shape[0], bands.shape[1], bands.shape[2]
    assert plan.shape[0] == 2 and 8 % planes == 0
    for rows in (52, 56, 60, 64):
        if points == 128 and count * rows % plane_count == 0 and rows % (count * rows // plane_count) == 0:
            units = count * rows // plane_count
            if units * planes % 8 == 0:
                break
    pack = Packing(points, rows)
    slots = pack.table.shape[1]
    width = 2 * slots
    vmem = pl.BlockSpec(memory_space=pltpu.VMEM)

    own_index = plan % count
    owner_group = plan // count
    if band_count == 2:
        met = lax.ppermute(bands, "band", [(0, 1), (1, 0)])
        met_index = own_index
    else:
        met = jnp.stack(
            [
                spread(lax.dynamic_index_in_dim(bands, own_index[turn], 0, False), "band", owner_group[turn])
                for turn in range(2)
            ]
        )
        met_index = jnp.arange(2, dtype=jnp.int32)
    mine = (owner_group == lax.axis_index("band")).astype(jnp.int32)
    units_each = rows // units
    quarter = lax.axis_index("plane").astype(jnp.int32)[None] % units_each
    info = jnp.concatenate([own_index, mine, met_index, quarter]).astype(jnp.int32)
    smem = pl.BlockSpec(memory_space=pltpu.SMEM)

    def pair(block):
        empty = np.zeros_like(block)
        return np.block([[block, empty], [empty, block]])

    z_high, z_low = split_host(pack.ztable)
    y_high, y_low = split_host(pack.ytable)
    forward_z = jnp.asarray(np.concatenate([pair(z_high), pair(z_low)], 1))
    forward_y = jnp.asarray(np.block([[y_high, y_high], [y_low, np.zeros_like(y_low)]]))
    owner = jnp.asarray(pack.owner)

    group = 8 // planes
    place = np.zeros((group * slots, plane_count * 8), np.float64)
    for item in range(group):
        for source in range(plane_count):
            for plane in range(planes):
                place[item * slots : (item + 1) * slots, source * 8 + item * planes + plane] = pack.table[
                    source * planes + plane
                ]
    x_high, x_low = split_host(place)
    forward_x = jnp.asarray(np.block([[x_high, x_high], [x_low, np.zeros_like(x_low)]]))
    backward_x = jnp.asarray(np.concatenate([x_high.T, x_high.T, x_low.T], 1))
    lanes = jnp.asarray(pack.lanes.reshape(units_each, units, width))
    wave = jnp.asarray(np.tile(pack.squares[:, None], (1, width)))

    backward_y = jnp.asarray(np.block([[y_high.T, y_high.T], [y_low.T, np.zeros_like(y_low.T)]]))
    back_high, back_low = pair(z_high.T), pair(z_low.T)
    backward_z = jnp.asarray(np.concatenate([back_high, back_high], 0))
    loaded = load(
        [bands, forward_z, forward_y, owner]
        + [lanes, wave, forward_x, backward_x]
        + [backward_y, backward_z, jnp.asarray(back_low), jnp.asarray(pack.came)]
    )
    loaded = [in_vmem(v) for v in loaded]
    bands_near, owner = loaded[0], loaded[3]
    sent, partner, lanes = pl.pallas_call(
        functools.partial(forward_kernel, pack=pack, step=planes),
        out_shape=(
            pltpu.VMEM((count, rows * planes, width), f32),
            pltpu.VMEM((2, planes, points, points), f32),
            pltpu.VMEM((units, width), f32),
        ),
        in_specs=[smem] + [vmem] * 6,
        out_specs=(vmem, vmem, vmem),
        compiler_params=pltpu.CompilerParams(vmem_limit_bytes=vmem_bytes),
        name="forward",
    )(info, bands_near, in_vmem(met), *loaded[1:5])

    lines = units * planes
    got = lax.all_to_all(
        sent.reshape(plane_count, lines, width), "plane", split_axis=0, concat_axis=0, tiled=True
    )

    back = pl.pallas_call(
        functools.partial(middle_kernel, planes=planes, points=points),
        out_shape=pltpu.VMEM((plane_count, lines, width), f32),
        in_specs=[vmem] * 5,
        out_specs=vmem,
        compiler_params=pltpu.CompilerParams(vmem_limit_bytes=vmem_bytes),
        name="middle",
    )(in_vmem(got), in_vmem(lanes), *loaded[5:8])
    home = lax.all_to_all(back, "plane", split_axis=0, concat_axis=0, tiled=True)
    home = home.reshape(count, rows * planes, width)

    return pl.pallas_call(
        functools.partial(backward_kernel, pack=pack, step=planes),
        out_shape=jax.ShapeDtypeStruct(bands.shape, f32),
        grid=(count,),
        in_specs=[vmem] * 7,
        out_specs=pl.BlockSpec((1, planes, points, points), lambda i: (i, 0, 0, 0)),
        compiler_params=pltpu.CompilerParams(vmem_limit_bytes=vmem_bytes),
        name="backward",
    )(in_vmem(home), in_vmem(partner), *loaded[8:11], owner, loaded[11])


def solution(mesh):
    in_specs = (P("band", "plane", None, None), P())
    out_specs = P("band", "plane", None, None)
    body = functools.partial(
        per_device, band_count=mesh.shape["band"], plane_count=mesh.shape["plane"]
    )
    return jax.shard_map(
        body, mesh=mesh, in_specs=in_specs, out_specs=out_specs, check_vma=False
    )
```

```python
import functools
import math

import jax
import jax.numpy as jnp
import numpy as np
from jax import lax
from jax.experimental import pallas as pl
from jax.experimental.pallas import tpu as pltpu
from jax.sharding import PartitionSpec as P

screening = 0.1
f32 = jnp.float32
bf16 = jnp.bfloat16
vmem_bytes = 24 << 20


def spread(value, axis, source):
    kept = jnp.where(lax.axis_index(axis) == source, value, 0).astype(value.dtype)
    return lax.psum(kept, axis)


def split_host(table):
    high = table.astype(jnp.bfloat16)
    low = (table - high.astype(np.float64)).astype(jnp.bfloat16)
    return high, low


def split(value):
    high = value.astype(bf16)
    return high, (value - high.astype(f32)).astype(bf16)


def dot(left, right):
    return jnp.dot(left, right, preferred_element_type=f32)


def basis(points):
    cutoff = points // 4
    grid = np.arange(points)
    waves = [k for k in range(1, cutoff) for _ in (0, 1)] + [0]
    table = np.zeros((points, 2 * cutoff), np.float64)
    for column, k in enumerate(waves):
        angles = 2.0 * math.pi * (k * grid % points) / points
        values = np.sin(angles) if column % 2 else np.cos(angles)
        table[:, column] = values * math.sqrt((1.0 if k == 0 else 2.0) / points)
    return table, waves


class Packing:
    def __init__(self, points, rows):
        table, waves = basis(points)
        cutoff = points // 4
        slots = 2 * cutoff
        order = sorted(range(slots - 1), key=lambda f: waves[f])
        self.ztable = np.concatenate([table[:, order], np.zeros((points, 1))], 1)
        zsquares = np.array([float(waves[f] ** 2) for f in order] + [np.inf])
        used = lambda k: int(np.sum(zsquares + k * k < cutoff**2))
        pairs = cutoff - 1 if rows == slots else (rows - 1) // 2
        self.rows = rows
        self.tall = tall = -(-rows // 8)
        base = lambda h: min(8 * h, rows - 8)
        self.base = base
        spot = lambda row: (row // 8, row - base(row // 8))
        far = float(points * points)
        squares = np.full((rows, slots), far)
        host = np.zeros((8 * tall,), np.int64) - 1
        owner = np.full((8 * tall, slots), -1)
        free = []

        def place(function, row, start, length, at):
            squares[row, at : at + length] = waves[function] ** 2 + zsquares[start : start + length]

        def settle(function, row):
            h, s = spot(row)
            host[8 * h + s] = function
            length = used(waves[function])
            owner[8 * h + s, :length] = 0
            place(function, row, 0, length, 0)
            return length

        for k in range(1, pairs + 1):
            for part in (0, 1):
                length = settle(2 * k - 2 + part, 2 * k - 2 + part)
            free.append([2 * k - 2, length, slots - length])
        settle(slots - 2, 2 * pairs)
        blank = 2 * pairs + 1 if 2 * pairs + 1 < rows else None

        extra = []
        moves = {}
        cells = []

        def move(function, row, start, at, length):
            h, s = spot(row)
            for e, held in enumerate(extra):
                if held[s] in (-1, function):
                    break
            else:
                e = len(extra)
                extra.append([-1] * 8)
            extra[e][s] = function
            number = moves.setdefault((e, h, (at - start) % (2 * slots)), len(moves) + 1)
            owner[8 * h + s, at : at + length] = number
            cells.append((number, e, s, start, length))
            place(function, row, start, length, at)

        rest = {k: [0, used(k)] for k in range(pairs + 1, cutoff)}

        def take(k, length, row, at, both):
            start = rest[k][0]
            for part in (0, 1):
                if both:
                    move(2 * k - 2 + part, row + part, start, at, length)
                else:
                    move(2 * k - 2 + part, row, start, at + part * (slots // 2), length)
            rest[k] = [start + length, rest[k][1] - length]
            if rest[k][1] == 0:
                del rest[k]

        gaps = [[length, row, at, True] for row, at, length in free]
        if blank is not None:
            gaps.append([slots // 2, blank, 0, False])
        gaps.sort(reverse=True)
        while rest:
            exact = [(g, k) for g in gaps for k in rest if rest[k][1] == g[0]]
            if exact:
                gap, k = exact[0]
            else:
                k = max(rest, key=lambda k: rest[k][1])
                whole = [g for g in gaps if g[0] >= rest[k][1]]
                gap = min(whole) if whole else gaps[0]
            length = min(gap[0], rest[k][1])
            take(k, length, gap[1], gap[2], gap[3])
            gap[0] -= length
            gap[2] += length
            gaps.sort(reverse=True)

        while (8 * tall + 8 * len(extra)) % 16:
            extra.append([-1] * 8)
        self.moves = [(number, e, h, shift) for (e, h, shift), number in moves.items()]
        self.extra = len(extra)
        came = np.full((8 * len(extra), slots), -1)
        for number, e, s, start, length in cells:
            came[8 * e + s, start : start + length] = number
        twice = lambda a: np.concatenate([a, a], 1)
        self.owner = twice(owner).astype(np.int32)
        self.came = twice(came).astype(np.int32) if extra else np.zeros((8, 2 * slots), np.int32)
        functions = list(host) + [f for held in extra for f in held]
        self.ytable = np.stack([table[:, f] if f >= 0 else np.zeros(points) for f in functions])
        self.lanes = twice(squares).astype(np.float32)
        self.table = table
        self.squares = np.array([float(k * k) for k in waves] + [far], np.float32)


def load_kernel(*refs):
    count = len(refs) // 2
    sems = refs[-1]
    copies = [
        pltpu.make_async_copy(source, target, sems.at[at])
        for at, (source, target) in enumerate(zip(refs[:count], refs[count : 2 * count]))
    ]
    for copy in copies:
        copy.start()
    for copy in copies:
        copy.wait()


def load(values):
    return pl.pallas_call(
        load_kernel,
        out_shape=tuple(pltpu.VMEM(v.shape, v.dtype) for v in values),
        in_specs=[pl.BlockSpec(memory_space=pltpu.HBM)] * len(values),
        out_specs=(pl.BlockSpec(memory_space=pltpu.VMEM),) * len(values),
        scratch_shapes=[pltpu.SemaphoreType.DMA((len(values),))],
        cost_estimate=pl.CostEstimate(
            flops=0, transcendentals=0, bytes_accessed=2 * sum(v.size * v.dtype.itemsize for v in values)
        ),
        compiler_params=pltpu.CompilerParams(vmem_limit_bytes=vmem_bytes),
        name="load",
    )(*[pltpu.with_memory_space_constraint(v, pltpu.HBM) for v in values])


def forward_kernel(info, bands, met, ztable, ytable, owner, lanes, out, partner, mine, *, pack, step):
    count, planes, points = bands.shape[:3]
    tall, width = ytable.shape[0] // 2, ztable.shape[1] // 2
    mine[...] = lanes[info[6]]
    for turn in range(2):
        @pl.when(info[2 + turn] == 1)
        def _():
            partner[turn] = bands[info[turn]]

        @pl.when(info[2 + turn] == 0)
        def _():
            partner[turn] = met[info[4 + turn]]

    def one(band, carry):
        for start in range(0, planes, step):
            here = bands[band, start : start + step]
            density = jnp.concatenate(
                [partner[0, start : start + step] * here, partner[1, start : start + step] * here], 2
            ).reshape(step * points, 2 * points)
            high, low = split(density)
            both = dot(high, ztable[...])
            lines = both[:, :width] + both[:, width:] + dot(low, ztable[:, :width])
            lines = jnp.concatenate([lines[at * points : (at + 1) * points] for at in range(step)], 1)
            high, low = split(lines)
            both = dot(ytable[...], jnp.concatenate([high, low], 0))
            columns = both[:tall] + both[tall:]
            for at in range(step):
                piece = columns[:, at * width : (at + 1) * width]
                host = [piece[8 * h : 8 * h + 8] for h in range(pack.tall)]
                more = [piece[8 * (pack.tall + e) : 8 * (pack.tall + e) + 8] for e in range(pack.extra)]
                for number, e, h, shift in pack.moves:
                    rolled = pltpu.roll(more[e], shift, 1) if shift else more[e]
                    host[h] = jnp.where(owner[8 * h : 8 * h + 8, :] == number, rolled, host[h])
                for h in reversed(range(pack.tall)):
                    first = pack.base(h) * planes + start + at
                    out[band, pl.ds(first, 8, stride=planes), :] = host[h]
        return carry

    lax.fori_loop(0, count, one, 0, unroll=4)


def middle_kernel(got, lanes, wave, xtable, xback, out, *, planes, points):
    group = 8 // planes
    tiles = got.shape[1] // 8
    kept = xtable.shape[0] // 2
    spacing = 2.0 * math.pi / points
    cutoff = float((points // 4) ** 2)
    width = got.shape[2]
    for first in range(0, tiles, 2):
        count = min(2, tiles - first)
        values = jnp.concatenate(
            [got[:, 8 * at : 8 * at + 8, :].reshape(-1, width) for at in range(first, first + count)], 1
        )
        high, low = split(values)
        both = dot(xtable[...], jnp.concatenate([high, low], 0))
        spectrum = both[:kept] + both[kept:]
        factor = []
        for at in range(first, first + count):
            parts = []
            for item in range(group):
                unit = at * group + item
                squared = wave[...] + lanes[unit : unit + 1, :]
                weight = 1.0 / (spacing * spacing * squared + screening * screening)
                parts.append(jnp.where(squared < cutoff, weight, 0.0))
            factor.append(parts[0] if group == 1 else jnp.concatenate(parts, 0))
        spectrum = spectrum * (factor[0] if count == 1 else jnp.concatenate(factor, 1))
        high, low = split(spectrum)
        back = dot(xback[...], jnp.concatenate([high, low, high], 0))
        for at in range(count):
            piece = back[:, at * width : (at + 1) * width]
            out[:, 8 * (first + at) : 8 * (first + at) + 8, :] = piece.reshape(-1, 8, width)


def backward_kernel(got, partner, yback, zback, zlow, owner, came, out, ready, sems, *, pack, step):
    count, planes, points = out.shape[:3]
    width = got.shape[2]
    copies = []

    def spectrum(band, plane):
        whole = [
            got[band, pl.ds(pack.base(h) * planes + plane, 8, stride=planes), :] for h in range(pack.tall)
        ]
        more = [jnp.zeros((8, width), f32) for _ in range(pack.extra)]
        for number, e, h, shift in pack.moves:
            rolled = pltpu.roll(whole[h], width - shift, 1) if shift else whole[h]
            more[e] = jnp.where(came[8 * e : 8 * e + 8, :] == number, rolled, more[e])
        host = [jnp.where(owner[8 * h : 8 * h + 8, :] == 0, whole[h], 0.0) for h in range(pack.tall)]
        return jnp.concatenate(host + more, 0)

    for band in range(count):
        for start in range(0, planes, step):
            columns = jnp.concatenate([spectrum(band, start + at) for at in range(step)], 1)
            high, low = split(columns)
            lines = dot(yback[...], jnp.concatenate([high, low], 0))
            lines = lines[:points] + lines[points:]
            lines = jnp.concatenate([lines[:, at * width : (at + 1) * width] for at in range(step)], 0)
            high, low = split(lines)
            waves = dot(jnp.concatenate([high, low], 1), zback[...]) + dot(high, zlow[...])
            waves = waves.reshape(step, points, 2 * points)
            ready[band, start : start + step] = -(
                partner[0, start : start + step] * waves[:, :, :points]
                + partner[1, start : start + step] * waves[:, :, points:]
            )
            here = (band, pl.ds(start, step))
            copies.append(pltpu.make_async_copy(ready.at[here], out.at[here], sems.at[len(copies)]))
            copies[-1].start()
    for copy in copies:
        copy.wait()


def in_vmem(value):
    return pltpu.with_memory_space_constraint(value, pltpu.VMEM)


def per_device(bands, plan, band_count, plane_count):
    count, planes, points = bands.shape[0], bands.shape[1], bands.shape[2]
    assert plan.shape[0] == 2 and 8 % planes == 0
    for rows in (52, 56, 60, 64):
        if points == 128 and count * rows % plane_count == 0 and rows % (count * rows // plane_count) == 0:
            units = count * rows // plane_count
            if units * planes % 8 == 0:
                break
    pack = Packing(points, rows)
    slots = pack.table.shape[1]
    width = 2 * slots
    vmem = pl.BlockSpec(memory_space=pltpu.VMEM)

    own_index = plan % count
    owner_group = plan // count
    if band_count == 2:
        met = lax.ppermute(bands, "band", [(0, 1), (1, 0)])
        met_index = own_index
    else:
        met = jnp.stack(
            [
                spread(lax.dynamic_index_in_dim(bands, own_index[turn], 0, False), "band", owner_group[turn])
                for turn in range(2)
            ]
        )
        met_index = jnp.arange(2, dtype=jnp.int32)
    mine = (owner_group == lax.axis_index("band")).astype(jnp.int32)
    units_each = rows // units
    quarter = lax.axis_index("plane").astype(jnp.int32)[None] % units_each
    info = jnp.concatenate([own_index, mine, met_index, quarter]).astype(jnp.int32)
    smem = pl.BlockSpec(memory_space=pltpu.SMEM)

    def pair(block):
        empty = np.zeros_like(block)
        return np.block([[block, empty], [empty, block]])

    z_high, z_low = split_host(pack.ztable)
    y_high, y_low = split_host(pack.ytable)
    forward_z = jnp.asarray(np.concatenate([pair(z_high), pair(z_low)], 1))
    forward_y = jnp.asarray(np.block([[y_high, y_high], [y_low, np.zeros_like(y_low)]]))
    owner = jnp.asarray(pack.owner)

    group = 8 // planes
    place = np.zeros((group * slots, plane_count * 8), np.float64)
    for item in range(group):
        for source in range(plane_count):
            for plane in range(planes):
                place[item * slots : (item + 1) * slots, source * 8 + item * planes + plane] = pack.table[
                    source * planes + plane
                ]
    x_high, x_low = split_host(place)
    forward_x = jnp.asarray(np.block([[x_high, x_high], [x_low, np.zeros_like(x_low)]]))
    backward_x = jnp.asarray(np.concatenate([x_high.T, x_high.T, x_low.T], 1))
    lanes = jnp.asarray(pack.lanes.reshape(units_each, units, width))
    wave = jnp.asarray(np.tile(pack.squares[:, None], (1, width)))

    backward_y = jnp.asarray(np.block([[y_high.T, y_high.T], [y_low.T, np.zeros_like(y_low.T)]]))
    back_high, back_low = pair(z_high.T), pair(z_low.T)
    backward_z = jnp.asarray(np.concatenate([back_high, back_high], 0))
    loaded = load(
        [bands, forward_z, forward_y, owner]
        + [lanes, wave, forward_x, backward_x]
        + [backward_y, backward_z, jnp.asarray(back_low), jnp.asarray(pack.came)]
    )
    loaded = [in_vmem(v) for v in loaded]
    bands_near, owner = loaded[0], loaded[3]
    sent, partner, lanes = pl.pallas_call(
        functools.partial(forward_kernel, pack=pack, step=planes),
        out_shape=(
            pltpu.VMEM((count, rows * planes, width), f32),
            pltpu.VMEM((2, planes, points, points), f32),
            pltpu.VMEM((units, width), f32),
        ),
        in_specs=[smem] + [vmem] * 6,
        out_specs=(vmem, vmem, vmem),
        compiler_params=pltpu.CompilerParams(vmem_limit_bytes=vmem_bytes),
        name="forward",
    )(info, bands_near, in_vmem(met), *loaded[1:5])

    lines = units * planes
    got = lax.all_to_all(
        sent.reshape(plane_count, lines, width), "plane", split_axis=0, concat_axis=0, tiled=True
    )

    back = pl.pallas_call(
        functools.partial(middle_kernel, planes=planes, points=points),
        out_shape=pltpu.VMEM((plane_count, lines, width), f32),
        in_specs=[vmem] * 5,
        out_specs=vmem,
        compiler_params=pltpu.CompilerParams(vmem_limit_bytes=vmem_bytes),
        name="middle",
    )(in_vmem(got), in_vmem(lanes), *loaded[5:8])
    home = lax.all_to_all(back, "plane", split_axis=0, concat_axis=0, tiled=True)
    home = home.reshape(count, rows * planes, width)

    return pl.pallas_call(
        functools.partial(backward_kernel, pack=pack, step=planes),
        out_shape=jax.ShapeDtypeStruct(bands.shape, f32),
        in_specs=[vmem] * 7,
        out_specs=pl.BlockSpec(memory_space=pltpu.HBM),
        scratch_shapes=[
            pltpu.VMEM(bands.shape, f32),
            pltpu.SemaphoreType.DMA((count,)),
        ],
        compiler_params=pltpu.CompilerParams(vmem_limit_bytes=vmem_bytes),
        name="backward",
    )(in_vmem(home), in_vmem(partner), *loaded[8:11], owner, loaded[11])


def solution(mesh):
    in_specs = (P("band", "plane", None, None), P())
    out_specs = P("band", "plane", None, None)
    body = functools.partial(
        per_device, band_count=mesh.shape["band"], plane_count=mesh.shape["plane"]
    )
    return jax.shard_map(
        body, mesh=mesh, in_specs=in_specs, out_specs=out_specs, check_vma=False
    )
```

```python
import functools
import math

import jax
import jax.numpy as jnp
import numpy as np
from jax import lax
from jax.experimental import pallas as pl
from jax.experimental.pallas import tpu as pltpu
from jax.sharding import PartitionSpec as P

screening = 0.1
f32 = jnp.float32
bf16 = jnp.bfloat16
vmem_bytes = 24 << 20


def spread(value, axis, source):
    kept = jnp.where(lax.axis_index(axis) == source, value, 0).astype(value.dtype)
    return lax.psum(kept, axis)


def split_host(table):
    high = table.astype(jnp.bfloat16)
    low = (table - high.astype(np.float64)).astype(jnp.bfloat16)
    return high, low


def split(value):
    high = value.astype(bf16)
    return high, (value - high.astype(f32)).astype(bf16)


def dot(left, right):
    return jnp.dot(left, right, preferred_element_type=f32)


def basis(points):
    cutoff = points // 4
    grid = np.arange(points)
    waves = [k for k in range(1, cutoff) for _ in (0, 1)] + [0]
    table = np.zeros((points, 2 * cutoff), np.float64)
    for column, k in enumerate(waves):
        angles = 2.0 * math.pi * (k * grid % points) / points
        values = np.sin(angles) if column % 2 else np.cos(angles)
        table[:, column] = values * math.sqrt((1.0 if k == 0 else 2.0) / points)
    return table, waves


class Packing:
    def __init__(self, points, rows):
        table, waves = basis(points)
        cutoff = points // 4
        slots = 2 * cutoff
        order = sorted(range(slots - 1), key=lambda f: waves[f])
        self.ztable = np.concatenate([table[:, order], np.zeros((points, 1))], 1)
        zsquares = np.array([float(waves[f] ** 2) for f in order] + [np.inf])
        used = lambda k: int(np.sum(zsquares + k * k < cutoff**2))
        pairs = cutoff - 1 if rows == slots else (rows - 1) // 2
        self.rows = rows
        self.tall = tall = -(-rows // 8)
        base = lambda h: min(8 * h, rows - 8)
        self.base = base
        spot = lambda row: (row // 8, row - base(row // 8))
        far = float(points * points)
        squares = np.full((rows, slots), far)
        host = np.zeros((8 * tall,), np.int64) - 1
        owner = np.full((8 * tall, slots), -1)
        free = []

        def place(function, row, start, length, at):
            squares[row, at : at + length] = waves[function] ** 2 + zsquares[start : start + length]

        def settle(function, row):
            h, s = spot(row)
            host[8 * h + s] = function
            length = used(waves[function])
            owner[8 * h + s, :length] = 0
            place(function, row, 0, length, 0)
            return length

        for k in range(1, pairs + 1):
            for part in (0, 1):
                length = settle(2 * k - 2 + part, 2 * k - 2 + part)
            free.append([2 * k - 2, length, slots - length])
        settle(slots - 2, 2 * pairs)
        blank = 2 * pairs + 1 if 2 * pairs + 1 < rows else None

        extra = []
        moves = {}
        cells = []

        def move(function, row, start, at, length):
            h, s = spot(row)
            for e, held in enumerate(extra):
                if held[s] in (-1, function):
                    break
            else:
                e = len(extra)
                extra.append([-1] * 8)
            extra[e][s] = function
            number = moves.setdefault((e, h, (at - start) % (2 * slots)), len(moves) + 1)
            owner[8 * h + s, at : at + length] = number
            cells.append((number, e, s, start, length))
            place(function, row, start, length, at)

        rest = {k: [0, used(k)] for k in range(pairs + 1, cutoff)}

        def take(k, length, row, at, both):
            start = rest[k][0]
            for part in (0, 1):
                if both:
                    move(2 * k - 2 + part, row + part, start, at, length)
                else:
                    move(2 * k - 2 + part, row, start, at + part * (slots // 2), length)
            rest[k] = [start + length, rest[k][1] - length]
            if rest[k][1] == 0:
                del rest[k]

        gaps = [[length, row, at, True] for row, at, length in free]
        if blank is not None:
            gaps.append([slots // 2, blank, 0, False])
        gaps.sort(reverse=True)
        while rest:
            exact = [(g, k) for g in gaps for k in rest if rest[k][1] == g[0]]
            if exact:
                gap, k = exact[0]
            else:
                k = max(rest, key=lambda k: rest[k][1])
                whole = [g for g in gaps if g[0] >= rest[k][1]]
                gap = min(whole) if whole else gaps[0]
            length = min(gap[0], rest[k][1])
            take(k, length, gap[1], gap[2], gap[3])
            gap[0] -= length
            gap[2] += length
            gaps.sort(reverse=True)

        while (8 * tall + 8 * len(extra)) % 16:
            extra.append([-1] * 8)
        self.moves = [(number, e, h, shift) for (e, h, shift), number in moves.items()]
        self.extra = len(extra)
        came = np.full((8 * len(extra), slots), -1)
        for number, e, s, start, length in cells:
            came[8 * e + s, start : start + length] = number
        twice = lambda a: np.concatenate([a, a], 1)
        self.owner = twice(owner).astype(np.int32)
        self.came = twice(came).astype(np.int32) if extra else np.zeros((8, 2 * slots), np.int32)
        functions = list(host) + [f for held in extra for f in held]
        self.ytable = np.stack([table[:, f] if f >= 0 else np.zeros(points) for f in functions])
        self.lanes = twice(squares).astype(np.float32)
        self.table = table
        self.squares = np.array([float(k * k) for k in waves] + [far], np.float32)


def load_kernel(*refs):
    count = len(refs) // 2
    sems = refs[-1]
    copies = [
        pltpu.make_async_copy(source, target, sems.at[at])
        for at, (source, target) in enumerate(zip(refs[:count], refs[count : 2 * count]))
    ]
    for copy in copies:
        copy.start()
    for copy in copies:
        copy.wait()


def load(values):
    return pl.pallas_call(
        load_kernel,
        out_shape=tuple(pltpu.VMEM(v.shape, v.dtype) for v in values),
        in_specs=[pl.BlockSpec(memory_space=pltpu.HBM)] * len(values),
        out_specs=(pl.BlockSpec(memory_space=pltpu.VMEM),) * len(values),
        scratch_shapes=[pltpu.SemaphoreType.DMA((len(values),))],
        cost_estimate=pl.CostEstimate(
            flops=0, transcendentals=0, bytes_accessed=2 * sum(v.size * v.dtype.itemsize for v in values)
        ),
        compiler_params=pltpu.CompilerParams(vmem_limit_bytes=vmem_bytes),
        name="load",
    )(*[pltpu.with_memory_space_constraint(v, pltpu.HBM) for v in values])


def forward_kernel(info, bands, met, ztable, ytable, owner, lanes, out, partner, mine, *, pack, step):
    count, planes, points = bands.shape[:3]
    tall, width = ytable.shape[0] // 2, ztable.shape[1] // 2
    mine[...] = lanes[info[6]]
    for turn in range(2):
        @pl.when(info[2 + turn] == 1)
        def _():
            partner[turn] = bands[info[turn]]

        @pl.when(info[2 + turn] == 0)
        def _():
            partner[turn] = met[info[4 + turn]]

    def first(band, start):
        here = bands[band, start : start + step]
        density = jnp.concatenate(
            [partner[0, start : start + step] * here, partner[1, start : start + step] * here], 2
        ).reshape(step * points, 2 * points)
        high, low = split(density)
        both = dot(high, ztable[...])
        lines = both[:, :width] + both[:, width:] + dot(low, ztable[:, :width])
        return split(jnp.concatenate([lines[at * points : (at + 1) * points] for at in range(step)], 1))

    def second(band, start, high, low):
        both = dot(ytable[...], jnp.concatenate([high, low], 0))
        columns = both[:tall] + both[tall:]
        for at in range(step):
            piece = columns[:, at * width : (at + 1) * width]
            host = [piece[8 * h : 8 * h + 8] for h in range(pack.tall)]
            more = [piece[8 * (pack.tall + e) : 8 * (pack.tall + e) + 8] for e in range(pack.extra)]
            for number, e, h, shift in pack.moves:
                rolled = pltpu.roll(more[e], shift, 1) if shift else more[e]
                host[h] = jnp.where(owner[8 * h : 8 * h + 8, :] == number, rolled, host[h])
            for h in reversed(range(pack.tall)):
                where = pack.base(h) * planes + start + at
                out[band, pl.ds(where, 8, stride=planes), :] = host[h]

    tasks = [(band, start) for band in range(count) for start in range(0, planes, step)]
    waiting = []
    for task in tasks:
        waiting.append((*task, *first(*task)))
        if len(waiting) > 1:
            second(*waiting.pop(0))
    for held in waiting:
        second(*held)


def middle_kernel(got, lanes, wave, xtable, xback, out, *, planes, points):
    group = 8 // planes
    tiles = got.shape[1] // 8
    kept = xtable.shape[0] // 2
    spacing = 2.0 * math.pi / points
    cutoff = float((points // 4) ** 2)
    width = got.shape[2]
    for first in range(0, tiles, 2):
        count = min(2, tiles - first)
        values = jnp.concatenate(
            [got[:, 8 * at : 8 * at + 8, :].reshape(-1, width) for at in range(first, first + count)], 1
        )
        high, low = split(values)
        both = dot(xtable[...], jnp.concatenate([high, low], 0))
        spectrum = both[:kept] + both[kept:]
        factor = []
        for at in range(first, first + count):
            parts = []
            for item in range(group):
                unit = at * group + item
                squared = wave[...] + lanes[unit : unit + 1, :]
                weight = 1.0 / (spacing * spacing * squared + screening * screening)
                parts.append(jnp.where(squared < cutoff, weight, 0.0))
            factor.append(parts[0] if group == 1 else jnp.concatenate(parts, 0))
        spectrum = spectrum * (factor[0] if count == 1 else jnp.concatenate(factor, 1))
        high, low = split(spectrum)
        back = dot(xback[...], jnp.concatenate([high, low, high], 0))
        for at in range(count):
            piece = back[:, at * width : (at + 1) * width]
            out[:, 8 * (first + at) : 8 * (first + at) + 8, :] = piece.reshape(-1, 8, width)


def backward_kernel(got, partner, yback, zback, zlow, owner, came, out, ready, sems, *, pack, step):
    count, planes, points = out.shape[:3]
    width = got.shape[2]
    copies = []

    def spectrum(band, plane):
        whole = [
            got[band, pl.ds(pack.base(h) * planes + plane, 8, stride=planes), :] for h in range(pack.tall)
        ]
        more = [jnp.zeros((8, width), f32) for _ in range(pack.extra)]
        for number, e, h, shift in pack.moves:
            rolled = pltpu.roll(whole[h], width - shift, 1) if shift else whole[h]
            more[e] = jnp.where(came[8 * e : 8 * e + 8, :] == number, rolled, more[e])
        host = [jnp.where(owner[8 * h : 8 * h + 8, :] == 0, whole[h], 0.0) for h in range(pack.tall)]
        return jnp.concatenate(host + more, 0)

    def first(band, start):
        columns = jnp.concatenate([spectrum(band, start + at) for at in range(step)], 1)
        high, low = split(columns)
        lines = dot(yback[...], jnp.concatenate([high, low], 0))
        lines = lines[:points] + lines[points:]
        return split(jnp.concatenate([lines[:, at * width : (at + 1) * width] for at in range(step)], 0))

    def second(band, start, high, low):
        waves = dot(jnp.concatenate([high, low], 1), zback[...]) + dot(high, zlow[...])
        waves = waves.reshape(step, points, 2 * points)
        ready[band, start : start + step] = -(
            partner[0, start : start + step] * waves[:, :, :points]
            + partner[1, start : start + step] * waves[:, :, points:]
        )
        here = (band, pl.ds(start, step))
        copies.append(pltpu.make_async_copy(ready.at[here], out.at[here], sems.at[len(copies)]))
        copies[-1].start()

    waiting = []
    for task in [(band, start) for band in range(count) for start in range(0, planes, step)]:
        waiting.append((*task, *first(*task)))
        if len(waiting) > 1:
            second(*waiting.pop(0))
    for held in waiting:
        second(*held)
    for copy in copies:
        copy.wait()


def in_vmem(value):
    return pltpu.with_memory_space_constraint(value, pltpu.VMEM)


def per_device(bands, plan, band_count, plane_count):
    count, planes, points = bands.shape[0], bands.shape[1], bands.shape[2]
    assert plan.shape[0] == 2 and 8 % planes == 0
    for rows in (52, 56, 60, 64):
        if points == 128 and count * rows % plane_count == 0 and rows % (count * rows // plane_count) == 0:
            units = count * rows // plane_count
            if units * planes % 8 == 0:
                break
    pack = Packing(points, rows)
    slots = pack.table.shape[1]
    width = 2 * slots
    vmem = pl.BlockSpec(memory_space=pltpu.VMEM)

    own_index = plan % count
    owner_group = plan // count
    if band_count == 2:
        met = lax.ppermute(bands, "band", [(0, 1), (1, 0)])
        met_index = own_index
    else:
        met = jnp.stack(
            [
                spread(lax.dynamic_index_in_dim(bands, own_index[turn], 0, False), "band", owner_group[turn])
                for turn in range(2)
            ]
        )
        met_index = jnp.arange(2, dtype=jnp.int32)
    mine = (owner_group == lax.axis_index("band")).astype(jnp.int32)
    units_each = rows // units
    quarter = lax.axis_index("plane").astype(jnp.int32)[None] % units_each
    info = jnp.concatenate([own_index, mine, met_index, quarter]).astype(jnp.int32)
    smem = pl.BlockSpec(memory_space=pltpu.SMEM)

    def pair(block):
        empty = np.zeros_like(block)
        return np.block([[block, empty], [empty, block]])

    z_high, z_low = split_host(pack.ztable)
    y_high, y_low = split_host(pack.ytable)
    forward_z = jnp.asarray(np.concatenate([pair(z_high), pair(z_low)], 1))
    forward_y = jnp.asarray(np.block([[y_high, y_high], [y_low, np.zeros_like(y_low)]]))
    owner = jnp.asarray(pack.owner)

    group = 8 // planes
    place = np.zeros((group * slots, plane_count * 8), np.float64)
    for item in range(group):
        for source in range(plane_count):
            for plane in range(planes):
                place[item * slots : (item + 1) * slots, source * 8 + item * planes + plane] = pack.table[
                    source * planes + plane
                ]
    x_high, x_low = split_host(place)
    forward_x = jnp.asarray(np.block([[x_high, x_high], [x_low, np.zeros_like(x_low)]]))
    backward_x = jnp.asarray(np.concatenate([x_high.T, x_high.T, x_low.T], 1))
    lanes = jnp.asarray(pack.lanes.reshape(units_each, units, width))
    wave = jnp.asarray(np.tile(pack.squares[:, None], (1, width)))

    backward_y = jnp.asarray(np.block([[y_high.T, y_high.T], [y_low.T, np.zeros_like(y_low.T)]]))
    back_high, back_low = pair(z_high.T), pair(z_low.T)
    backward_z = jnp.asarray(np.concatenate([back_high, back_high], 0))
    loaded = load(
        [bands, forward_z, forward_y, owner]
        + [lanes, wave, forward_x, backward_x]
        + [backward_y, backward_z, jnp.asarray(back_low), jnp.asarray(pack.came)]
    )
    loaded = [in_vmem(v) for v in loaded]
    bands_near, owner = loaded[0], loaded[3]
    sent, partner, lanes = pl.pallas_call(
        functools.partial(forward_kernel, pack=pack, step=planes),
        out_shape=(
            pltpu.VMEM((count, rows * planes, width), f32),
            pltpu.VMEM((2, planes, points, points), f32),
            pltpu.VMEM((units, width), f32),
        ),
        in_specs=[smem] + [vmem] * 6,
        out_specs=(vmem, vmem, vmem),
        compiler_params=pltpu.CompilerParams(vmem_limit_bytes=vmem_bytes),
        name="forward",
    )(info, bands_near, in_vmem(met), *loaded[1:5])

    lines = units * planes
    got = lax.all_to_all(
        sent.reshape(plane_count, lines, width), "plane", split_axis=0, concat_axis=0, tiled=True
    )

    back = pl.pallas_call(
        functools.partial(middle_kernel, planes=planes, points=points),
        out_shape=pltpu.VMEM((plane_count, lines, width), f32),
        in_specs=[vmem] * 5,
        out_specs=vmem,
        compiler_params=pltpu.CompilerParams(vmem_limit_bytes=vmem_bytes),
        name="middle",
    )(in_vmem(got), in_vmem(lanes), *loaded[5:8])
    home = lax.all_to_all(back, "plane", split_axis=0, concat_axis=0, tiled=True)
    home = home.reshape(count, rows * planes, width)

    return pl.pallas_call(
        functools.partial(backward_kernel, pack=pack, step=max(planes // 2, 1)),
        out_shape=jax.ShapeDtypeStruct(bands.shape, f32),
        in_specs=[vmem] * 7,
        out_specs=pl.BlockSpec(memory_space=pltpu.HBM),
        scratch_shapes=[
            pltpu.VMEM(bands.shape, f32),
            pltpu.SemaphoreType.DMA((2 * count,)),
        ],
        compiler_params=pltpu.CompilerParams(vmem_limit_bytes=vmem_bytes),
        name="backward",
    )(in_vmem(home), in_vmem(partner), *loaded[8:11], owner, loaded[11])


def solution(mesh):
    in_specs = (P("band", "plane", None, None), P())
    out_specs = P("band", "plane", None, None)
    body = functools.partial(
        per_device, band_count=mesh.shape["band"], plane_count=mesh.shape["plane"]
    )
    return jax.shard_map(
        body, mesh=mesh, in_specs=in_specs, out_specs=out_specs, check_vma=False
    )
```

```python
import functools
import math

import jax
import jax.numpy as jnp
import numpy as np
from jax import lax
from jax.experimental import pallas as pl
from jax.experimental.pallas import tpu as pltpu
from jax.sharding import PartitionSpec as P

screening = 0.1
f32 = jnp.float32
bf16 = jnp.bfloat16
vmem_bytes = 24 << 20


def spread(value, axis, source):
    kept = jnp.where(lax.axis_index(axis) == source, value, 0).astype(value.dtype)
    return lax.psum(kept, axis)


def split_host(table):
    high = table.astype(jnp.bfloat16)
    low = (table - high.astype(np.float64)).astype(jnp.bfloat16)
    return high, low


def split(value):
    high = value.astype(bf16)
    return high, (value - high.astype(f32)).astype(bf16)


def dot(left, right):
    return jnp.dot(left, right, preferred_element_type=f32)


def basis(points):
    cutoff = points // 4
    grid = np.arange(points)
    waves = [k for k in range(1, cutoff) for _ in (0, 1)] + [0]
    table = np.zeros((points, 2 * cutoff), np.float64)
    for column, k in enumerate(waves):
        angles = 2.0 * math.pi * (k * grid % points) / points
        values = np.sin(angles) if column % 2 else np.cos(angles)
        table[:, column] = values * math.sqrt((1.0 if k == 0 else 2.0) / points)
    return table, waves


class Packing:
    def __init__(self, points, rows):
        table, waves = basis(points)
        cutoff = points // 4
        slots = 2 * cutoff
        order = sorted(range(slots - 1), key=lambda f: waves[f])
        self.ztable = np.concatenate([table[:, order], np.zeros((points, 1))], 1)
        zsquares = np.array([float(waves[f] ** 2) for f in order] + [np.inf])
        used = lambda k: int(np.sum(zsquares + k * k < cutoff**2))
        pairs = cutoff - 1 if rows == slots else (rows - 1) // 2
        self.rows = rows
        self.tall = tall = -(-rows // 8)
        base = lambda h: min(8 * h, rows - 8)
        self.base = base
        spot = lambda row: (row // 8, row - base(row // 8))
        far = float(points * points)
        squares = np.full((rows, slots), far)
        host = np.zeros((8 * tall,), np.int64) - 1
        owner = np.full((8 * tall, slots), -1)
        free = []

        def place(function, row, start, length, at):
            squares[row, at : at + length] = waves[function] ** 2 + zsquares[start : start + length]

        def settle(function, row):
            h, s = spot(row)
            host[8 * h + s] = function
            length = used(waves[function])
            owner[8 * h + s, :length] = 0
            place(function, row, 0, length, 0)
            return length

        for k in range(1, pairs + 1):
            for part in (0, 1):
                length = settle(2 * k - 2 + part, 2 * k - 2 + part)
            free.append([2 * k - 2, length, slots - length])
        settle(slots - 2, 2 * pairs)
        blank = 2 * pairs + 1 if 2 * pairs + 1 < rows else None

        extra = []
        moves = {}
        cells = []

        def move(function, row, start, at, length):
            h, s = spot(row)
            for e, held in enumerate(extra):
                if held[s] in (-1, function):
                    break
            else:
                e = len(extra)
                extra.append([-1] * 8)
            extra[e][s] = function
            number = moves.setdefault((e, h, (at - start) % (2 * slots)), len(moves) + 1)
            owner[8 * h + s, at : at + length] = number
            cells.append((number, e, s, start, length))
            place(function, row, start, length, at)

        rest = {k: [0, used(k)] for k in range(pairs + 1, cutoff)}

        def take(k, length, row, at, both):
            start = rest[k][0]
            for part in (0, 1):
                if both:
                    move(2 * k - 2 + part, row + part, start, at, length)
                else:
                    move(2 * k - 2 + part, row, start, at + part * (slots // 2), length)
            rest[k] = [start + length, rest[k][1] - length]
            if rest[k][1] == 0:
                del rest[k]

        gaps = [[length, row, at, True] for row, at, length in free]
        if blank is not None:
            gaps.append([slots // 2, blank, 0, False])
        gaps.sort(reverse=True)
        while rest:
            exact = [(g, k) for g in gaps for k in rest if rest[k][1] == g[0]]
            if exact:
                gap, k = exact[0]
            else:
                k = max(rest, key=lambda k: rest[k][1])
                whole = [g for g in gaps if g[0] >= rest[k][1]]
                gap = min(whole) if whole else gaps[0]
            length = min(gap[0], rest[k][1])
            take(k, length, gap[1], gap[2], gap[3])
            gap[0] -= length
            gap[2] += length
            gaps.sort(reverse=True)

        while (8 * tall + 8 * len(extra)) % 16:
            extra.append([-1] * 8)
        self.moves = [(number, e, h, shift) for (e, h, shift), number in moves.items()]
        self.extra = len(extra)
        came = np.full((8 * len(extra), slots), -1)
        for number, e, s, start, length in cells:
            came[8 * e + s, start : start + length] = number
        twice = lambda a: np.concatenate([a, a], 1)
        self.owner = twice(owner).astype(np.int32)
        self.came = twice(came).astype(np.int32) if extra else np.zeros((8, 2 * slots), np.int32)
        functions = list(host) + [f for held in extra for f in held]
        self.ytable = np.stack([table[:, f] if f >= 0 else np.zeros(points) for f in functions])
        self.lanes = twice(squares).astype(np.float32)
        self.table = table
        self.squares = np.array([float(k * k) for k in waves] + [far], np.float32)


def load_kernel(*refs):
    count = len(refs) // 2
    sems = refs[-1]
    copies = [
        pltpu.make_async_copy(source, target, sems.at[at])
        for at, (source, target) in enumerate(zip(refs[:count], refs[count : 2 * count]))
    ]
    for copy in copies:
        copy.start()
    for copy in copies:
        copy.wait()


def load(values):
    return pl.pallas_call(
        load_kernel,
        out_shape=tuple(pltpu.VMEM(v.shape, v.dtype) for v in values),
        in_specs=[pl.BlockSpec(memory_space=pltpu.HBM)] * len(values),
        out_specs=(pl.BlockSpec(memory_space=pltpu.VMEM),) * len(values),
        scratch_shapes=[pltpu.SemaphoreType.DMA((len(values),))],
        cost_estimate=pl.CostEstimate(
            flops=0, transcendentals=0, bytes_accessed=2 * sum(v.size * v.dtype.itemsize for v in values)
        ),
        compiler_params=pltpu.CompilerParams(vmem_limit_bytes=vmem_bytes),
        name="load",
    )(*[pltpu.with_memory_space_constraint(v, pltpu.HBM) for v in values])


def forward_kernel(info, bands, met, ztable, ytable, owner, lanes, out, partner, mine, *, pack, step):
    count, planes, points = bands.shape[:3]
    tall, width = ytable.shape[0] // 2, ztable.shape[1] // 2
    mine[...] = lanes[info[6]]
    for turn in range(2):
        @pl.when(info[2 + turn] == 1)
        def _():
            partner[turn] = bands[info[turn]]

        @pl.when(info[2 + turn] == 0)
        def _():
            partner[turn] = met[info[4 + turn]]

    def first(band, start):
        here = bands[band, start : start + step]
        density = jnp.concatenate(
            [partner[0, start : start + step] * here, partner[1, start : start + step] * here], 2
        ).reshape(step * points, 2 * points)
        high, low = split(density)
        both = dot(high, ztable[...])
        lines = both[:, :width] + both[:, width:] + dot(low, ztable[:, :width])
        return split(jnp.concatenate([lines[at * points : (at + 1) * points] for at in range(step)], 1))

    def second(band, start, high, low):
        both = dot(ytable[...], jnp.concatenate([high, low], 0))
        columns = both[:tall] + both[tall:]
        for at in range(step):
            piece = columns[:, at * width : (at + 1) * width]
            host = [piece[8 * h : 8 * h + 8] for h in range(pack.tall)]
            more = [piece[8 * (pack.tall + e) : 8 * (pack.tall + e) + 8] for e in range(pack.extra)]
            for number, e, h, shift in pack.moves:
                rolled = pltpu.roll(more[e], shift, 1) if shift else more[e]
                host[h] = jnp.where(owner[8 * h : 8 * h + 8, :] == number, rolled, host[h])
            for h in reversed(range(pack.tall)):
                where = pack.base(h) * planes + start + at
                out[band, pl.ds(where, 8, stride=planes), :] = host[h]

    tasks = [(band, start) for band in range(count) for start in range(0, planes, step)]
    waiting = []
    for task in tasks:
        waiting.append((*task, *first(*task)))
        if len(waiting) > 1:
            second(*waiting.pop(0))
    for held in waiting:
        second(*held)


def middle_kernel(got, lanes, wave, xtable, xback, out, *, planes, points):
    group = 8 // planes
    tiles = got.shape[1] // 8
    kept = xtable.shape[0] // 2
    spacing = 2.0 * math.pi / points
    cutoff = float((points // 4) ** 2)
    width = got.shape[2]
    def ahead():
        mine = range(tiles)
        values = jnp.concatenate([got[:, 8 * at : 8 * at + 8, :].reshape(-1, width) for at in mine], 1)
        high, low = split(values)
        both = dot(xtable[...], jnp.concatenate([high, low], 0))
        spectrum = both[:kept] + both[kept:]
        factor = []
        for at in mine:
            parts = []
            for item in range(group):
                unit = at * group + item
                squared = wave[...] + lanes[unit : unit + 1, :]
                weight = 1.0 / (spacing * spacing * squared + screening * screening)
                parts.append(jnp.where(squared < cutoff, weight, 0.0))
            factor.append(parts[0] if group == 1 else jnp.concatenate(parts, 0))
        return mine, split(spectrum * (factor[0] if len(mine) == 1 else jnp.concatenate(factor, 1)))

    def behind(mine, parts):
        high, low = parts
        back = dot(xback[...], jnp.concatenate([high, low, high], 0))
        for place, at in enumerate(mine):
            piece = back[:, place * width : (place + 1) * width]
            out[:, 8 * at : 8 * at + 8, :] = piece.reshape(-1, 8, width)

    behind(*ahead())


def backward_kernel(got, partner, yback, zback, zlow, owner, came, out, ready, sems, *, pack, step):
    count, planes, points = out.shape[:3]
    width = got.shape[2]
    copies = []

    def spectrum(band, plane):
        whole = [
            got[band, pl.ds(pack.base(h) * planes + plane, 8, stride=planes), :] for h in range(pack.tall)
        ]
        more = [jnp.zeros((8, width), f32) for _ in range(pack.extra)]
        for number, e, h, shift in pack.moves:
            rolled = pltpu.roll(whole[h], width - shift, 1) if shift else whole[h]
            more[e] = jnp.where(came[8 * e : 8 * e + 8, :] == number, rolled, more[e])
        host = [jnp.where(owner[8 * h : 8 * h + 8, :] == 0, whole[h], 0.0) for h in range(pack.tall)]
        return jnp.concatenate(host + more, 0)

    def first(band, start):
        columns = jnp.concatenate([spectrum(band, start + at) for at in range(step)], 1)
        high, low = split(columns)
        lines = dot(yback[...], jnp.concatenate([high, low], 0))
        lines = lines[:points] + lines[points:]
        return split(jnp.concatenate([lines[:, at * width : (at + 1) * width] for at in range(step)], 0))

    def second(band, start, high, low):
        waves = dot(jnp.concatenate([high, low], 1), zback[...]) + dot(high, zlow[...])
        waves = waves.reshape(step, points, 2 * points)
        ready[band, start : start + step] = -(
            partner[0, start : start + step] * waves[:, :, :points]
            + partner[1, start : start + step] * waves[:, :, points:]
        )
        here = (band, pl.ds(start, step))
        copies.append(pltpu.make_async_copy(ready.at[here], out.at[here], sems.at[len(copies)]))
        copies[-1].start()

    waiting = []
    for task in [(band, start) for band in range(count) for start in range(0, planes, step)]:
        waiting.append((*task, *first(*task)))
        if len(waiting) > 1:
            second(*waiting.pop(0))
    for held in waiting:
        second(*held)
    for copy in copies:
        copy.wait()


def in_vmem(value):
    return pltpu.with_memory_space_constraint(value, pltpu.VMEM)


def per_device(bands, plan, band_count, plane_count):
    count, planes, points = bands.shape[0], bands.shape[1], bands.shape[2]
    assert plan.shape[0] == 2 and 8 % planes == 0
    for rows in (52, 56, 60, 64):
        if points == 128 and count * rows % plane_count == 0 and rows % (count * rows // plane_count) == 0:
            units = count * rows // plane_count
            if units * planes % 8 == 0:
                break
    pack = Packing(points, rows)
    slots = pack.table.shape[1]
    width = 2 * slots
    vmem = pl.BlockSpec(memory_space=pltpu.VMEM)

    own_index = plan % count
    owner_group = plan // count
    if band_count == 2:
        met = lax.ppermute(bands, "band", [(0, 1), (1, 0)])
        met_index = own_index
    else:
        met = jnp.stack(
            [
                spread(lax.dynamic_index_in_dim(bands, own_index[turn], 0, False), "band", owner_group[turn])
                for turn in range(2)
            ]
        )
        met_index = jnp.arange(2, dtype=jnp.int32)
    mine = (owner_group == lax.axis_index("band")).astype(jnp.int32)
    units_each = rows // units
    quarter = lax.axis_index("plane").astype(jnp.int32)[None] % units_each
    info = jnp.concatenate([own_index, mine, met_index, quarter]).astype(jnp.int32)
    smem = pl.BlockSpec(memory_space=pltpu.SMEM)

    def pair(block):
        empty = np.zeros_like(block)
        return np.block([[block, empty], [empty, block]])

    z_high, z_low = split_host(pack.ztable)
    y_high, y_low = split_host(pack.ytable)
    forward_z = jnp.asarray(np.concatenate([pair(z_high), pair(z_low)], 1))
    forward_y = jnp.asarray(np.block([[y_high, y_high], [y_low, np.zeros_like(y_low)]]))
    owner = jnp.asarray(pack.owner)

    group = 8 // planes
    place = np.zeros((group * slots, plane_count * 8), np.float64)
    for item in range(group):
        for source in range(plane_count):
            for plane in range(planes):
                place[item * slots : (item + 1) * slots, source * 8 + item * planes + plane] = pack.table[
                    source * planes + plane
                ]
    x_high, x_low = split_host(place)
    forward_x = jnp.asarray(np.block([[x_high, x_high], [x_low, np.zeros_like(x_low)]]))
    backward_x = jnp.asarray(np.concatenate([x_high.T, x_high.T, x_low.T], 1))
    lanes = jnp.asarray(pack.lanes.reshape(units_each, units, width))
    wave = jnp.asarray(np.tile(pack.squares[:, None], (1, width)))

    backward_y = jnp.asarray(np.block([[y_high.T, y_high.T], [y_low.T, np.zeros_like(y_low.T)]]))
    back_high, back_low = pair(z_high.T), pair(z_low.T)
    backward_z = jnp.asarray(np.concatenate([back_high, back_high], 0))
    loaded = load(
        [bands, forward_z, forward_y, owner]
        + [lanes, wave, forward_x, backward_x]
        + [backward_y, backward_z, jnp.asarray(back_low), jnp.asarray(pack.came)]
    )
    loaded = [in_vmem(v) for v in loaded]
    bands_near, owner = loaded[0], loaded[3]
    sent, partner, lanes = pl.pallas_call(
        functools.partial(forward_kernel, pack=pack, step=planes),
        out_shape=(
            pltpu.VMEM((count, rows * planes, width), f32),
            pltpu.VMEM((2, planes, points, points), f32),
            pltpu.VMEM((units, width), f32),
        ),
        in_specs=[smem] + [vmem] * 6,
        out_specs=(vmem, vmem, vmem),
        compiler_params=pltpu.CompilerParams(vmem_limit_bytes=vmem_bytes),
        name="forward",
    )(info, bands_near, in_vmem(met), *loaded[1:5])

    lines = units * planes
    got = lax.all_to_all(
        sent.reshape(plane_count, lines, width), "plane", split_axis=0, concat_axis=0, tiled=True
    )

    back = pl.pallas_call(
        functools.partial(middle_kernel, planes=planes, points=points),
        out_shape=pltpu.VMEM((plane_count, lines, width), f32),
        in_specs=[vmem] * 5,
        out_specs=vmem,
        compiler_params=pltpu.CompilerParams(vmem_limit_bytes=vmem_bytes),
        name="middle",
    )(in_vmem(got), in_vmem(lanes), *loaded[5:8])
    home = lax.all_to_all(back, "plane", split_axis=0, concat_axis=0, tiled=True)
    home = home.reshape(count, rows * planes, width)

    return pl.pallas_call(
        functools.partial(backward_kernel, pack=pack, step=max(planes // 2, 1)),
        out_shape=jax.ShapeDtypeStruct(bands.shape, f32),
        in_specs=[vmem] * 7,
        out_specs=pl.BlockSpec(memory_space=pltpu.HBM),
        scratch_shapes=[
            pltpu.VMEM(bands.shape, f32),
            pltpu.SemaphoreType.DMA((2 * count,)),
        ],
        compiler_params=pltpu.CompilerParams(vmem_limit_bytes=vmem_bytes),
        name="backward",
    )(in_vmem(home), in_vmem(partner), *loaded[8:11], owner, loaded[11])


def solution(mesh):
    in_specs = (P("band", "plane", None, None), P())
    out_specs = P("band", "plane", None, None)
    body = functools.partial(
        per_device, band_count=mesh.shape["band"], plane_count=mesh.shape["plane"]
    )
    return jax.shard_map(
        body, mesh=mesh, in_specs=in_specs, out_specs=out_specs, check_vma=False
    )
```

```python
import functools
import math

import jax
import jax.numpy as jnp
import numpy as np
from jax import lax
from jax.experimental import pallas as pl
from jax.experimental.pallas import tpu as pltpu
from jax.sharding import PartitionSpec as P

screening = 0.1
f32 = jnp.float32
bf16 = jnp.bfloat16
vmem_bytes = 24 << 20


def spread(value, axis, source):
    kept = jnp.where(lax.axis_index(axis) == source, value, 0).astype(value.dtype)
    return lax.psum(kept, axis)


def split_host(table):
    high = table.astype(jnp.bfloat16)
    low = (table - high.astype(np.float64)).astype(jnp.bfloat16)
    return high, low


def split(value):
    high = value.astype(bf16)
    return high, (value - high.astype(f32)).astype(bf16)


def dot(left, right):
    return jnp.dot(left, right, preferred_element_type=f32)


def basis(points):
    cutoff = points // 4
    grid = np.arange(points)
    waves = [k for k in range(1, cutoff) for _ in (0, 1)] + [0]
    table = np.zeros((points, 2 * cutoff), np.float64)
    for column, k in enumerate(waves):
        angles = 2.0 * math.pi * (k * grid % points) / points
        values = np.sin(angles) if column % 2 else np.cos(angles)
        table[:, column] = values * math.sqrt((1.0 if k == 0 else 2.0) / points)
    return table, waves


class Packing:
    def __init__(self, points, rows):
        table, waves = basis(points)
        cutoff = points // 4
        slots = 2 * cutoff
        order = sorted(range(slots - 1), key=lambda f: waves[f])
        self.ztable = np.concatenate([table[:, order], np.zeros((points, 1))], 1)
        zsquares = np.array([float(waves[f] ** 2) for f in order] + [np.inf])
        used = lambda k: int(np.sum(zsquares + k * k < cutoff**2))
        pairs = cutoff - 1 if rows == slots else (rows - 1) // 2
        self.rows = rows
        self.tall = tall = -(-rows // 8)
        base = lambda h: min(8 * h, rows - 8)
        self.base = base
        spot = lambda row: (row // 8, row - base(row // 8))
        far = float(points * points)
        squares = np.full((rows, slots), far)
        host = np.zeros((8 * tall,), np.int64) - 1
        owner = np.full((8 * tall, slots), -1)
        free = []

        def place(function, row, start, length, at):
            squares[row, at : at + length] = waves[function] ** 2 + zsquares[start : start + length]

        def settle(function, row):
            h, s = spot(row)
            host[8 * h + s] = function
            length = used(waves[function])
            owner[8 * h + s, :length] = 0
            place(function, row, 0, length, 0)
            return length

        for k in range(1, pairs + 1):
            for part in (0, 1):
                length = settle(2 * k - 2 + part, 2 * k - 2 + part)
            free.append([2 * k - 2, length, slots - length])
        settle(slots - 2, 2 * pairs)
        blank = 2 * pairs + 1 if 2 * pairs + 1 < rows else None

        extra = []
        moves = {}
        cells = []

        def move(function, row, start, at, length):
            h, s = spot(row)
            for e, held in enumerate(extra):
                if held[s] in (-1, function):
                    break
            else:
                e = len(extra)
                extra.append([-1] * 8)
            extra[e][s] = function
            number = moves.setdefault((e, h, (at - start) % (2 * slots)), len(moves) + 1)
            owner[8 * h + s, at : at + length] = number
            cells.append((number, e, s, start, length))
            place(function, row, start, length, at)

        rest = {k: [0, used(k)] for k in range(pairs + 1, cutoff)}

        def take(k, length, row, at, both):
            start = rest[k][0]
            for part in (0, 1):
                if both:
                    move(2 * k - 2 + part, row + part, start, at, length)
                else:
                    move(2 * k - 2 + part, row, start, at + part * (slots // 2), length)
            rest[k] = [start + length, rest[k][1] - length]
            if rest[k][1] == 0:
                del rest[k]

        gaps = [[length, row, at, True] for row, at, length in free]
        if blank is not None:
            gaps.append([slots // 2, blank, 0, False])
        gaps.sort(reverse=True)
        while rest:
            exact = [(g, k) for g in gaps for k in rest if rest[k][1] == g[0]]
            if exact:
                gap, k = exact[0]
            else:
                k = max(rest, key=lambda k: rest[k][1])
                whole = [g for g in gaps if g[0] >= rest[k][1]]
                gap = min(whole) if whole else gaps[0]
            length = min(gap[0], rest[k][1])
            take(k, length, gap[1], gap[2], gap[3])
            gap[0] -= length
            gap[2] += length
            gaps.sort(reverse=True)

        while (8 * tall + 8 * len(extra)) % 16:
            extra.append([-1] * 8)
        self.moves = [(number, e, h, shift) for (e, h, shift), number in moves.items()]
        self.extra = len(extra)
        came = np.full((8 * len(extra), slots), -1)
        for number, e, s, start, length in cells:
            came[8 * e + s, start : start + length] = number
        twice = lambda a: np.concatenate([a, a], 1)
        self.owner = twice(owner).astype(np.int32)
        self.came = twice(came).astype(np.int32) if extra else np.zeros((8, 2 * slots), np.int32)
        functions = list(host) + [f for held in extra for f in held]
        self.ytable = np.stack([table[:, f] if f >= 0 else np.zeros(points) for f in functions])
        self.lanes = twice(squares).astype(np.float32)
        self.table = table
        self.squares = np.array([float(k * k) for k in waves] + [far], np.float32)


def load_kernel(*refs):
    count = len(refs) // 2
    sems = refs[-1]
    copies = [
        pltpu.make_async_copy(source, target, sems.at[at])
        for at, (source, target) in enumerate(zip(refs[:count], refs[count : 2 * count]))
    ]
    for copy in copies:
        copy.start()
    for copy in copies:
        copy.wait()


def load(values):
    return pl.pallas_call(
        load_kernel,
        out_shape=tuple(pltpu.VMEM(v.shape, v.dtype) for v in values),
        in_specs=[pl.BlockSpec(memory_space=pltpu.HBM)] * len(values),
        out_specs=(pl.BlockSpec(memory_space=pltpu.VMEM),) * len(values),
        scratch_shapes=[pltpu.SemaphoreType.DMA((len(values),))],
        cost_estimate=pl.CostEstimate(
            flops=0, transcendentals=0, bytes_accessed=2 * sum(v.size * v.dtype.itemsize for v in values)
        ),
        compiler_params=pltpu.CompilerParams(vmem_limit_bytes=vmem_bytes),
        name="load",
    )(*[pltpu.with_memory_space_constraint(v, pltpu.HBM) for v in values])


def forward_kernel(info, bands, met, ztable, ytable, owner, lanes, out, partner, mine, *, pack, step):
    count, planes, points = bands.shape[:3]
    tall, width = ytable.shape[0] // 2, ztable.shape[1] // 2
    mine[...] = lanes[info[6]]
    for turn in range(2):
        @pl.when(info[2 + turn] == 1)
        def _():
            partner[turn] = bands[info[turn]]

        @pl.when(info[2 + turn] == 0)
        def _():
            partner[turn] = met[info[4 + turn]]

    def first(band, start):
        here = bands[band, start : start + step]
        density = jnp.concatenate(
            [partner[0, start : start + step] * here, partner[1, start : start + step] * here], 2
        ).reshape(step * points, 2 * points)
        high, low = split(density)
        both = dot(high, ztable[...])
        lines = both[:, :width] + both[:, width:] + dot(low, ztable[:, :width])
        return split(jnp.concatenate([lines[at * points : (at + 1) * points] for at in range(step)], 1))

    def second(band, start, high, low):
        both = dot(ytable[...], jnp.concatenate([high, low], 0))
        columns = both[:tall] + both[tall:]
        for at in range(step):
            piece = columns[:, at * width : (at + 1) * width]
            host = [piece[8 * h : 8 * h + 8] for h in range(pack.tall)]
            more = [piece[8 * (pack.tall + e) : 8 * (pack.tall + e) + 8] for e in range(pack.extra)]
            for number, e, h, shift in pack.moves:
                rolled = pltpu.roll(more[e], shift, 1) if shift else more[e]
                host[h] = jnp.where(owner[8 * h : 8 * h + 8, :] == number, rolled, host[h])
            for h in reversed(range(pack.tall)):
                where = pack.base(h) * planes + start + at
                out[band, pl.ds(where, 8, stride=planes), :] = host[h]

    tasks = [(band, start) for band in range(count) for start in range(0, planes, step)]
    waiting = []
    for task in tasks:
        waiting.append((*task, *first(*task)))
        if len(waiting) > 1:
            second(*waiting.pop(0))
    for held in waiting:
        second(*held)


def middle_kernel(got, lanes, wave, xtable, xback, out, *, planes, points):
    group = 8 // planes
    tiles = got.shape[1] // 8
    kept = xtable.shape[0] // 2
    spacing = 2.0 * math.pi / points
    cutoff = float((points // 4) ** 2)
    width = got.shape[2]
    def ahead():
        mine = range(tiles)
        values = jnp.concatenate([got[:, 8 * at : 8 * at + 8, :].reshape(-1, width) for at in mine], 1)
        high, low = split(values)
        both = dot(xtable[...], jnp.concatenate([high, low], 0))
        spectrum = both[:kept] + both[kept:]
        factor = []
        for at in mine:
            parts = []
            for item in range(group):
                unit = at * group + item
                squared = wave[...] + lanes[unit : unit + 1, :]
                weight = 1.0 / (spacing * spacing * squared + screening * screening)
                parts.append(jnp.where(squared < cutoff, weight, 0.0))
            factor.append(parts[0] if group == 1 else jnp.concatenate(parts, 0))
        return mine, split(spectrum * (factor[0] if len(mine) == 1 else jnp.concatenate(factor, 1)))

    def behind(mine, parts):
        high, low = parts
        back = dot(xback[...], jnp.concatenate([high, low, high], 0))
        for place, at in enumerate(mine):
            piece = back[:, place * width : (place + 1) * width]
            out[:, 8 * at : 8 * at + 8, :] = piece.reshape(-1, 8, width)

    behind(*ahead())


def backward_kernel(got, partner, yback, zback, zlow, owner, came, out, ready, sems, *, pack, step):
    count, planes, points = out.shape[:3]
    width = got.shape[2]
    copies = []

    def spectrum(band, plane):
        whole = [
            got[band, pl.ds(pack.base(h) * planes + plane, 8, stride=planes), :] for h in range(pack.tall)
        ]
        more = [jnp.zeros((8, width), f32) for _ in range(pack.extra)]
        for number, e, h, shift in pack.moves:
            rolled = pltpu.roll(whole[h], width - shift, 1) if shift else whole[h]
            more[e] = jnp.where(came[8 * e : 8 * e + 8, :] == number, rolled, more[e])
        host = [jnp.where(owner[8 * h : 8 * h + 8, :] == 0, whole[h], 0.0) for h in range(pack.tall)]
        return jnp.concatenate(host + more, 0)

    def first(band, start):
        columns = jnp.concatenate([spectrum(band, start + at) for at in range(step)], 1)
        high, low = split(columns)
        lines = dot(yback[...], jnp.concatenate([high, low], 0))
        lines = lines[:points] + lines[points:]
        return split(jnp.concatenate([lines[:, at * width : (at + 1) * width] for at in range(step)], 0))

    def second(band, start, high, low):
        waves = dot(jnp.concatenate([high, low], 1), zback[...]) + dot(high, zlow[...])
        waves = waves.reshape(step, points, 2 * points)
        ready[band, start : start + step] = (
            partner[0, start : start + step] * waves[:, :, :points]
            + partner[1, start : start + step] * waves[:, :, points:]
        )
        here = (band, pl.ds(start, step))
        copies.append(pltpu.make_async_copy(ready.at[here], out.at[here], sems.at[len(copies)]))
        copies[-1].start()

    waiting = []
    for task in [(band, start) for band in range(count) for start in range(0, planes, step)]:
        waiting.append((*task, *first(*task)))
        if len(waiting) > 1:
            second(*waiting.pop(0))
    for held in waiting:
        second(*held)
    for copy in copies:
        copy.wait()


def in_vmem(value):
    return pltpu.with_memory_space_constraint(value, pltpu.VMEM)


def per_device(bands, plan, band_count, plane_count):
    count, planes, points = bands.shape[0], bands.shape[1], bands.shape[2]
    assert plan.shape[0] == 2 and 8 % planes == 0
    for rows in (52, 56, 60, 64):
        if points == 128 and count * rows % plane_count == 0 and rows % (count * rows // plane_count) == 0:
            units = count * rows // plane_count
            if units * planes % 8 == 0:
                break
    pack = Packing(points, rows)
    slots = pack.table.shape[1]
    width = 2 * slots
    vmem = pl.BlockSpec(memory_space=pltpu.VMEM)

    own_index = plan % count
    owner_group = plan // count
    if band_count == 2:
        met = lax.ppermute(bands, "band", [(0, 1), (1, 0)])
        met_index = own_index
    else:
        met = jnp.stack(
            [
                spread(lax.dynamic_index_in_dim(bands, own_index[turn], 0, False), "band", owner_group[turn])
                for turn in range(2)
            ]
        )
        met_index = jnp.arange(2, dtype=jnp.int32)
    mine = (owner_group == lax.axis_index("band")).astype(jnp.int32)
    units_each = rows // units
    quarter = lax.axis_index("plane").astype(jnp.int32)[None] % units_each
    info = jnp.concatenate([own_index, mine, met_index, quarter]).astype(jnp.int32)
    smem = pl.BlockSpec(memory_space=pltpu.SMEM)

    def pair(block):
        empty = np.zeros_like(block)
        return np.block([[block, empty], [empty, block]])

    z_high, z_low = split_host(pack.ztable)
    y_high, y_low = split_host(pack.ytable)
    forward_z = jnp.asarray(np.concatenate([pair(z_high), pair(z_low)], 1))
    forward_y = jnp.asarray(np.block([[y_high, y_high], [y_low, np.zeros_like(y_low)]]))
    owner = jnp.asarray(pack.owner)

    group = 8 // planes
    place = np.zeros((group * slots, plane_count * 8), np.float64)
    for item in range(group):
        for source in range(plane_count):
            for plane in range(planes):
                place[item * slots : (item + 1) * slots, source * 8 + item * planes + plane] = pack.table[
                    source * planes + plane
                ]
    x_high, x_low = split_host(place)
    forward_x = jnp.asarray(np.block([[x_high, x_high], [x_low, np.zeros_like(x_low)]]))
    backward_x = jnp.asarray(np.concatenate([x_high.T, x_high.T, x_low.T], 1))
    lanes = jnp.asarray(pack.lanes.reshape(units_each, units, width))
    wave = jnp.asarray(np.tile(pack.squares[:, None], (1, width)))

    backward_y = jnp.asarray(np.block([[y_high.T, y_high.T], [y_low.T, np.zeros_like(y_low.T)]]))
    back_high, back_low = -pair(z_high.T), -pair(z_low.T)
    backward_z = jnp.asarray(np.concatenate([back_high, back_high], 0))
    loaded = load(
        [bands, forward_z, forward_y, owner]
        + [lanes, wave, forward_x, backward_x]
        + [backward_y, backward_z, jnp.asarray(back_low), jnp.asarray(pack.came)]
    )
    loaded = [in_vmem(v) for v in loaded]
    bands_near, owner = loaded[0], loaded[3]
    sent, partner, lanes = pl.pallas_call(
        functools.partial(forward_kernel, pack=pack, step=planes),
        out_shape=(
            pltpu.VMEM((count, rows * planes, width), f32),
            pltpu.VMEM((2, planes, points, points), f32),
            pltpu.VMEM((units, width), f32),
        ),
        in_specs=[smem] + [vmem] * 6,
        out_specs=(vmem, vmem, vmem),
        compiler_params=pltpu.CompilerParams(vmem_limit_bytes=vmem_bytes),
        name="forward",
    )(info, bands_near, in_vmem(met), *loaded[1:5])

    lines = units * planes
    got = lax.all_to_all(
        sent.reshape(plane_count, lines, width), "plane", split_axis=0, concat_axis=0, tiled=True
    )

    back = pl.pallas_call(
        functools.partial(middle_kernel, planes=planes, points=points),
        out_shape=pltpu.VMEM((plane_count, lines, width), f32),
        in_specs=[vmem] * 5,
        out_specs=vmem,
        compiler_params=pltpu.CompilerParams(vmem_limit_bytes=vmem_bytes),
        name="middle",
    )(in_vmem(got), in_vmem(lanes), *loaded[5:8])
    home = lax.all_to_all(back, "plane", split_axis=0, concat_axis=0, tiled=True)
    home = home.reshape(count, rows * planes, width)

    return pl.pallas_call(
        functools.partial(backward_kernel, pack=pack, step=max(planes // 2, 1)),
        out_shape=jax.ShapeDtypeStruct(bands.shape, f32),
        in_specs=[vmem] * 7,
        out_specs=pl.BlockSpec(memory_space=pltpu.HBM),
        scratch_shapes=[
            pltpu.VMEM(bands.shape, f32),
            pltpu.SemaphoreType.DMA((2 * count,)),
        ],
        compiler_params=pltpu.CompilerParams(vmem_limit_bytes=vmem_bytes),
        name="backward",
    )(in_vmem(home), in_vmem(partner), *loaded[8:11], owner, loaded[11])


def solution(mesh):
    in_specs = (P("band", "plane", None, None), P())
    out_specs = P("band", "plane", None, None)
    body = functools.partial(
        per_device, band_count=mesh.shape["band"], plane_count=mesh.shape["plane"]
    )
    return jax.shard_map(
        body, mesh=mesh, in_specs=in_specs, out_specs=out_specs, check_vma=False
    )
```
